32 devices in a mesh: clip: 16 (over z, y, core), frame: 2 (over x).
Axes of the slice: x: 2, y: 2, z: 4, core: 2. Of those that a mesh axis runs over, the one named last changes fastest.
Arguments:
- patch_tokens: bfloat16 [2, 32, 8, 196, 768], P(None, 'clip', 'frame'), may hold values from -6 to 6
- live_slots: int32 [2, 16], P(None, 'clip'), may hold values from 1 to 2, 24 in all within a row
- out_grad: bfloat16 [2, 32, 8, 196, 768], P(None, 'clip', 'frame'), may hold values from -6 to 6
- temporal_gain: bfloat16 [768], P(('clip', 'frame')), may hold values from 0.5 to 1.5
- temporal_shift: bfloat16 [768], P(('clip', 'frame')), may hold values from -1.75 to 1.75
- temporal_in: bfloat16 [768, 2304], P(('clip', 'frame')), may hold values from -0.21875 to 0.21875
- temporal_out: bfloat16 [768, 768], P(('clip', 'frame')), may hold values from -0.4375 to 0.4375
- temporal_bias: bfloat16 [768], P(('clip', 'frame')), may hold values from -1.75 to 1.75
- spatial_gain: bfloat16 [768], P(('clip', 'frame')), may hold values from 0.5 to 1.5
- spatial_shift: bfloat16 [768], P(('clip', 'frame')), may hold values from -1.75 to 1.75
- spatial_in: bfloat16 [768, 2304], P(('clip', 'frame')), may hold values from -0.21875 to 0.21875
- spatial_out: bfloat16 [768, 768], P(('clip', 'frame')), may hold values from -1.25 to 1.25
- spatial_bias: bfloat16 [768], P(('clip', 'frame')), may hold values from -1.75 to 1.75
- mlp_gain: bfloat16 [768], P(('clip', 'frame')), may hold values from 0.5 to 1.5
- mlp_shift: bfloat16 [768], P(('clip', 'frame')), may hold values from -1.75 to 1.75
- expand_weight: bfloat16 [768, 3072], P(('clip', 'frame')), may hold values from -0.21875 to 0.21875
- expand_bias: bfloat16 [3072], P(('clip', 'frame')), may hold values from -3 to 3
- shrink_weight: bfloat16 [3072, 768], P(('clip', 'frame')), may hold values from -0.109375 to 0.109375
- shrink_bias: bfloat16 [768], P(('clip', 'frame')), may hold values from -1.75 to 1.75
Outputs:
- block_out: bfloat16 [2, 32, 8, 196, 768], P(None, 'clip', 'frame')
- patch_grad: bfloat16 [2, 32, 8, 196, 768], P(None, 'clip', 'frame')
- g_temporal_gain: float32 [768], P(('clip', 'frame'))
- g_temporal_shift: float32 [768], P(('clip', 'frame'))
- g_temporal_in: float32 [768, 2304], P(('clip', 'frame'))
- g_temporal_out: float32 [768, 768], P(('clip', 'frame'))
- g_temporal_bias: float32 [768], P(('clip', 'frame'))
- g_spatial_gain: float32 [768], P(('clip', 'frame'))
- g_spatial_shift: float32 [768], P(('clip', 'frame'))
- g_spatial_in: float32 [768, 2304], P(('clip', 'frame'))
- g_spatial_out: float32 [768, 768], P(('clip', 'frame'))
- g_spatial_bias: float32 [768], P(('clip', 'frame'))
- g_mlp_gain: float32 [768], P(('clip', 'frame'))
- g_mlp_shift: float32 [768], P(('clip', 'frame'))
- g_expand_weight: float32 [768, 3072], P(('clip', 'frame'))
- g_expand_bias: float32 [3072], P(('clip', 'frame'))
- g_shrink_weight: float32 [3072, 768], P(('clip', 'frame'))
- g_shrink_bias: float32 [768], P(('clip', 'frame'))
The draws below stay inside these ranges and needn't reach their ends.
Inputs may be any that keep to these rules, and one draw needn't show every extreme that they name: `live_slots`: slot c of a group of clip holds a clip in micro-batch m if c is below the entry; each micro-batch holds 24 clips, and in each some group holds 2.
All inputs are finite; a program needn't handle non-finite values.
Results may differ from the reference program's by a relative error of at most 0.019.
Values may be sent and summed in bfloat16 or wider, within the bound.
A program may use at most 280 MiB of HBM per device.

```python
import math
import jax
import jax.numpy as jnp
import numpy as np
from jax import lax

D = 768
H = 12
DH = 64
FF = 3072
FRAMES = 8
PATCHES = 196
MB = 2
CAP = 2
SLOTS = 32
N_CLIP = 16


def level_of(stream_key, extent, cuts, low, top_value):
    level, own = 1.0, jax.random.fold_in(stream_key, 6)
    for axis_at, shards_of in cuts:
        steps = jnp.exp(jax.random.uniform(jax.random.fold_in(own, axis_at), (shards_of,), jnp.float32, low / len(cuts), top_value / len(cuts)))
        level = level * jnp.repeat(steps, extent[axis_at] // shards_of).reshape([-1 if axis == axis_at else 1 for axis in range(len(extent))])
    return level


def profile(number_of, total, most, lean):
    weights = [(1 << 20) // math.isqrt(rank ** lean) + 1 for rank in range(2, number_of + 1)]
    spare, holding = total - most - (number_of - 1), [1] * (number_of - 1)
    while spare > 0:
        free = [i for i in range(number_of - 1) if holding[i] < most]
        mass, remaining = sum([weights[i] for i in free]), spare
        for i in free:
            extra = min(most - holding[i], max(1, remaining * weights[i] // mass), spare)
            holding[i] = holding[i] + extra
            spare = spare - extra
    return np.array([most] + holding)


def ragged_sizes(rng, amount, total, reach, lean):
    if amount == 2:
        one = jax.random.randint(rng, (), max(1, total - reach), min(reach, total - 1) + 1)
        return jnp.stack([one, total - one])
    lengths = jnp.asarray(profile(amount, total, reach, lean), jnp.int32)
    twos = (amount - 1) // 2
    donor, taker = lengths[1:1 + 2 * twos:2], lengths[2:2 + 2 * twos:2]
    room = jnp.minimum(donor - 1, reach - taker)
    shifted = jax.random.randint(jax.random.fold_in(rng, 1), (twos,), 0, 1 << 20) % (room + 1)
    lengths = lengths.at[1:1 + 2 * twos:2].set(donor - shifted).at[2:2 + 2 * twos:2].set(taker + shifted)
    return lengths[jax.random.permutation(jax.random.fold_in(rng, 2), amount)]


def bell_draw(key, extent, deviation, most, pieces=(), kind=jnp.bfloat16):
    entries = jax.random.normal(key, extent, jnp.float32) * deviation
    if len(pieces) > 0:
        entries = level_of(key, extent, pieces, -0.22, 0.18) * entries
    return jnp.clip(entries, min=-most, max=most).astype(kind)


def setup_inputs(seed: int = 0) -> dict:
    keys = jax.random.split(jax.random.key(seed), 20)
    patch_tokens = bell_draw(keys[0], (MB, SLOTS, FRAMES, PATCHES, D), 1.0, 6.0, ((1, 16), (2, 2)))
    live_slots = jax.vmap(lambda own: ragged_sizes(own, N_CLIP, N_CLIP * CAP * 3 // 4, CAP, 1))(jax.random.split(keys[1], MB)).reshape((MB, N_CLIP)).astype(jnp.int32)
    out_grad = bell_draw(keys[2], (MB, SLOTS, FRAMES, PATCHES, D), 1.0, 6.0, ((1, 16), (2, 2)))
    temporal_gain = jnp.clip(1.0 + 0.1 * jax.random.normal(keys[3], (D,), jnp.float32), 0.5, 1.5).astype(jnp.bfloat16)
    temporal_shift = bell_draw(keys[4], (D,), 0.3, 1.75, ((0, 32),))
    temporal_in = bell_draw(keys[5], (D, 3 * D), D ** -0.5, 0.21875, ((0, 32),))
    temporal_out = bell_draw(keys[6], (D, D), (D // 4) ** -0.5, 0.4375, ((0, 32),))
    temporal_bias = bell_draw(keys[7], (D,), 0.3, 1.75, ((0, 32),))
    spatial_gain = jnp.clip(1.0 + 0.1 * jax.random.normal(keys[8], (D,), jnp.float32), 0.5, 1.5).astype(jnp.bfloat16)
    spatial_shift = bell_draw(keys[9], (D,), 0.3, 1.75, ((0, 32),))
    spatial_in = bell_draw(keys[10], (D, 3 * D), D ** -0.5, 0.21875, ((0, 32),))
    spatial_out = bell_draw(keys[11], (D, D), (D // 32) ** -0.5, 1.25, ((0, 32),))
    spatial_bias = bell_draw(keys[12], (D,), 0.3, 1.75, ((0, 32),))
    mlp_gain = jnp.clip(1.0 + 0.1 * jax.random.normal(keys[13], (D,), jnp.float32), 0.5, 1.5).astype(jnp.bfloat16)
    mlp_shift = bell_draw(keys[14], (D,), 0.3, 1.75, ((0, 32),))
    expand_weight = bell_draw(keys[15], (D, FF), D ** -0.5, 0.21875, ((0, 32),))
    expand_bias = bell_draw(keys[16], (FF,), 0.5, 3.0, ((0, 32),))
    shrink_weight = bell_draw(keys[17], (FF, D), FF ** -0.5, 0.109375, ((0, 32),))
    shrink_bias = bell_draw(keys[18], (D,), 0.3, 1.75, ((0, 32),))
    return dict(patch_tokens=patch_tokens, live_slots=live_slots, out_grad=out_grad, temporal_gain=temporal_gain, temporal_shift=temporal_shift, temporal_in=temporal_in, temporal_out=temporal_out, temporal_bias=temporal_bias, spatial_gain=spatial_gain, spatial_shift=spatial_shift, spatial_in=spatial_in, spatial_out=spatial_out, spatial_bias=spatial_bias, mlp_gain=mlp_gain, mlp_shift=mlp_shift, expand_weight=expand_weight, expand_bias=expand_bias, shrink_weight=shrink_weight, shrink_bias=shrink_bias)


exact_mode = lax.Precision.HIGHEST

@jax.custom_vjp
def low(v):
    return lax.optimization_barrier(v.astype(jnp.bfloat16)).astype(jnp.float32)

@jax.custom_vjp
def low_back(v):
    return v

def low_keep(v):
    return (low(v), None)

def low_pass(kept, grad):
    return (grad,)

def back_keep(v):
    return (v, None)

def back_low(kept, grad):
    return (low(grad),)
low.defvjp(low_keep, low_pass)
low_back.defvjp(back_keep, back_low)

def stored(values):
    return low_back(low(values))

def layer_norm(values, gain, shift):
    centre = values - lax.optimization_barrier(jnp.mean(values, -1, keepdims=True))
    spread = lax.optimization_barrier(jnp.mean(centre * centre, -1, keepdims=True))
    return centre * lax.rsqrt(spread + 1e-06) * gain + shift

def matmul(left, right):
    return jnp.dot(left, right, precision=exact_mode, preferred_element_type=jnp.float32)

def clip_forward(params, tokens):
    temporal_gain, temporal_shift, temporal_in, temporal_out, temporal_bias, spatial_gain, spatial_shift, spatial_in, spatial_out, spatial_bias, mlp_gain, mlp_shift, expand_weight, expand_bias, shrink_weight, shrink_bias = params
    head_shape = (FRAMES, PATCHES, H, DH)
    flat_in = tokens.reshape(FRAMES * PATCHES, D)
    normed_t = low(layer_norm(flat_in, temporal_gain, temporal_shift))
    packed_t = matmul(normed_t, temporal_in)
    query_t = stored(packed_t[:, :D]).reshape(head_shape)
    key_t = stored(packed_t[:, D:2 * D]).reshape(head_shape)
    value_t = stored(packed_t[:, 2 * D:]).reshape(head_shape)
    scores_t = low_back(jnp.einsum('fphd,gphd->phfg', query_t, key_t, precision=exact_mode) * 0.125)
    probs_t = low(jax.nn.softmax(scores_t, axis=-1))
    mixed_t = stored(jnp.einsum('phfg,gphd->fphd', probs_t, value_t, precision=exact_mode).reshape(FRAMES * PATCHES, D))
    after_time = flat_in + low_back(matmul(mixed_t, temporal_out) + temporal_bias)
    normed_s = low(layer_norm(after_time, spatial_gain, spatial_shift))
    packed_s = matmul(normed_s, spatial_in)
    query_s = stored(packed_s[:, :D]).reshape(head_shape)
    key_s = stored(packed_s[:, D:2 * D]).reshape(head_shape)
    value_s = stored(packed_s[:, 2 * D:]).reshape(head_shape)
    scores_s = low_back(jnp.einsum('fphd,frhd->fhpr', query_s, key_s, precision=exact_mode) * 0.125)
    probs_s = low(jax.nn.softmax(scores_s, axis=-1))
    mixed_s = stored(jnp.einsum('fhpr,frhd->fphd', probs_s, value_s, precision=exact_mode).reshape(FRAMES * PATCHES, D))
    after_space = after_time + low_back(matmul(mixed_s, spatial_out) + spatial_bias)
    normed_m = low(layer_norm(after_space, mlp_gain, mlp_shift))
    hidden = low_back(matmul(normed_m, expand_weight) + expand_bias)
    active = low(jax.nn.gelu(hidden, approximate=False))
    result = after_space + low_back(matmul(active, shrink_weight) + shrink_bias)
    return result.reshape(FRAMES, PATCHES, D)

def reference(patch_tokens, live_slots, out_grad, temporal_gain, temporal_shift, temporal_in, temporal_out, temporal_bias, spatial_gain, spatial_shift, spatial_in, spatial_out, spatial_bias, mlp_gain, mlp_shift, expand_weight, expand_bias, shrink_weight, shrink_bias):
    params = tuple((member.astype(jnp.float32) for member in (temporal_gain, temporal_shift, temporal_in, temporal_out, temporal_bias, spatial_gain, spatial_shift, spatial_in, spatial_out, spatial_bias, mlp_gain, mlp_shift, expand_weight, expand_bias, shrink_weight, shrink_bias)))
    inputs = patch_tokens.astype(jnp.float32).reshape(MB * SLOTS, FRAMES, PATCHES, D)
    live_mask = (jnp.arange(CAP, dtype=jnp.int32)[None, None, :] < live_slots[:, :, None]).astype(jnp.float32)
    live_mask = live_mask.reshape(MB * SLOTS, 1, 1, 1)
    cotan = out_grad.astype(jnp.float32).reshape(MB * SLOTS, FRAMES, PATCHES, D) * live_mask

    def forward(weights_all, clips_all):
        return lax.map(jax.checkpoint(lambda one_clip: clip_forward(weights_all, one_clip)), clips_all)
    outputs, backward = jax.vjp(forward, params, inputs)
    param_grads, input_grads = backward(cotan)
    full_shape = (MB, SLOTS, FRAMES, PATCHES, D)
    return (outputs.reshape(full_shape).astype(jnp.bfloat16), input_grads.reshape(full_shape).astype(jnp.bfloat16), param_grads[0], param_grads[1], param_grads[2], param_grads[3], param_grads[4], param_grads[5], param_grads[6], param_grads[7], param_grads[8], param_grads[9], param_grads[10], param_grads[11], param_grads[12], param_grads[13], param_grads[14], param_grads[15])
```

```python
import jax
import jax.numpy as jnp
from jax import lax
from jax.experimental import pallas as pl
from jax.experimental.pallas import tpu as pltpu
from jax.sharding import PartitionSpec as P

H = 12
DH = 64
D = 768
PATCHES = 196
ROWS = 208
PAIR = 2
HALF = 4
TILE = PAIR * ROWS
GROUP = 3
CHUNK = 768
CHUNKS = 4
BLOCK = 16
BLOCKS = ROWS // BLOCK
VMEM_BYTES = 66 * 1000 * 1000
bf16 = jnp.bfloat16
f32 = jnp.float32


def layer_norm(values, gain, shift):
    centre = values - jnp.mean(values, -1, keepdims=True)
    spread = jnp.mean(centre * centre, -1, keepdims=True)
    return centre * lax.rsqrt(spread + 1e-06) * gain + shift


def exact_gelu(values):
    return jax.nn.gelu(values, approximate=False)


def rows_product(left, right):
    return lax.dot_general(
        left, right, (((0,), (0,)), ((), ())), preferred_element_type=jnp.float32
    )


def back_product(grads_in, weight):
    return lax.dot_general(
        grads_in, weight, (((1,), (1,)), ((), ())), preferred_element_type=jnp.float32
    )


def forward_dot(left, right):
    return jnp.dot(left, right, preferred_element_type=jnp.float32)


def softmax_parts(scores):
    top_value = jnp.max(scores, -1, keepdims=True)
    expo_value = jnp.exp(scores - top_value)
    total_value = jnp.sum(expo_value, -1, keepdims=True)
    return (expo_value / total_value, top_value + jnp.log(total_value))


def softmax_back(probs, grad_probs):
    return (probs * (grad_probs - jnp.sum(probs * grad_probs, -1, keepdims=True))).astype(
        jnp.bfloat16
    )


def to_patch_rows(values, slot_count, local_frames, patch_count):
    width = values.shape[-1]
    return (
        values.reshape(slot_count, local_frames, patch_count, width)
        .transpose(0, 2, 1, 3)
        .reshape(slot_count * patch_count, local_frames, width)
    )


def from_patch_rows(values, slot_count, local_frames, patch_count):
    width = values.shape[-1]
    return (
        values.reshape(slot_count, patch_count, local_frames, width)
        .transpose(0, 2, 1, 3)
        .reshape(slot_count * local_frames * patch_count, width)
    )


def micro_batch(weights, tokens, out_cot, count):
    (
        temporal_gain,
        temporal_shift,
        temporal_in,
        temporal_out,
        temporal_bias,
        spatial_gain,
        spatial_shift,
        spatial_in,
        spatial_out,
        spatial_bias,
        mlp_gain,
        mlp_shift,
        expand_weight,
        expand_bias,
        shrink_weight,
        shrink_bias,
    ) = weights
    slot_count, local_frames, patch_count, model_width = tokens.shape
    row_count = slot_count * local_frames * patch_count
    head_shape = (slot_count, local_frames, patch_count, H, DH)
    live_mask = (jnp.arange(slot_count) < count).astype(jnp.float32)[:, None, None, None]
    cotan = (out_cot.astype(jnp.float32) * live_mask).reshape(row_count, model_width)
    flat_in = tokens.astype(jnp.float32).reshape(row_count, model_width)
    normed_t, norm_t_back = jax.vjp(
        layer_norm, flat_in, temporal_gain.astype(jnp.float32), temporal_shift.astype(jnp.float32)
    )
    normed_t = normed_t.astype(jnp.bfloat16)
    packed_t = forward_dot(normed_t, temporal_in).astype(jnp.bfloat16)
    frame_rows = lax.all_to_all(
        to_patch_rows(packed_t, slot_count, local_frames, patch_count),
        "frame",
        split_axis=0,
        concat_axis=1,
        tiled=True,
    )
    row_part, all_frames = (frame_rows.shape[0], frame_rows.shape[1])
    split_shape = (row_part, all_frames, H, DH)
    query_x = frame_rows[:, :, :model_width].reshape(split_shape)
    key_x = frame_rows[:, :, model_width : 2 * model_width].reshape(split_shape)
    value_x = frame_rows[:, :, 2 * model_width :].reshape(split_shape)
    scores_x = (
        jnp.einsum("rfhd,rghd->rhfg", query_x, key_x, preferred_element_type=jnp.float32) * 0.125
    )
    probs_x, lse_x = softmax_parts(scores_x)
    mixed_x = jnp.einsum(
        "rhfg,rghd->rfhd", probs_x.astype(jnp.bfloat16), value_x, preferred_element_type=jnp.float32
    )
    mixed_x = mixed_x.astype(jnp.bfloat16).reshape(row_part, all_frames, model_width)
    mixed_back = lax.all_to_all(mixed_x, "frame", split_axis=1, concat_axis=0, tiled=True)
    mixed_t = from_patch_rows(mixed_back, slot_count, local_frames, patch_count)
    after_time = flat_in + forward_dot(mixed_t, temporal_out) + temporal_bias.astype(jnp.float32)
    normed_s, norm_s_back = jax.vjp(
        layer_norm, after_time, spatial_gain.astype(jnp.float32), spatial_shift.astype(jnp.float32)
    )
    normed_s = normed_s.astype(jnp.bfloat16)
    packed_s = (
        forward_dot(normed_s, spatial_in)
        .astype(jnp.bfloat16)
        .reshape(slot_count, local_frames, patch_count, 3, H, DH)
    )
    query_s = packed_s[:, :, :, 0]
    key_s = packed_s[:, :, :, 1]
    value_s = packed_s[:, :, :, 2]
    scores_s = (
        jnp.einsum("cfphd,cfrhd->cfhpr", query_s, key_s, preferred_element_type=jnp.float32) * 0.125
    )
    probs_s, lse_s = softmax_parts(scores_s)
    mixed_s = jnp.einsum(
        "cfhpr,cfrhd->cfphd",
        probs_s.astype(jnp.bfloat16),
        value_s,
        preferred_element_type=jnp.float32,
    )
    mixed_s = mixed_s.astype(jnp.bfloat16).reshape(row_count, model_width)
    after_space = after_time + forward_dot(mixed_s, spatial_out) + spatial_bias.astype(jnp.float32)
    normed_m, norm_m_back = jax.vjp(
        layer_norm, after_space, mlp_gain.astype(jnp.float32), mlp_shift.astype(jnp.float32)
    )
    normed_m = normed_m.astype(jnp.bfloat16)
    hidden = forward_dot(normed_m, expand_weight) + expand_bias.astype(jnp.float32)
    active, gelu_back = jax.vjp(exact_gelu, hidden)
    active = active.astype(jnp.bfloat16)
    block_rows = after_space + forward_dot(active, shrink_weight) + shrink_bias.astype(jnp.float32)
    grad_z = cotan.astype(jnp.bfloat16)
    g_shrink_weight = rows_product(active, grad_z)
    g_shrink_bias = jnp.sum(grad_z.astype(jnp.float32), 0)
    grad_hidden = gelu_back(back_product(grad_z, shrink_weight))[0].astype(jnp.bfloat16)
    g_expand_weight = rows_product(normed_m, grad_hidden)
    g_expand_bias = jnp.sum(grad_hidden.astype(jnp.float32), 0)
    space_grad, g_mlp_gain, g_mlp_shift = norm_m_back(back_product(grad_hidden, expand_weight))
    space_grad = cotan + space_grad
    grad_ys = space_grad.astype(jnp.bfloat16)
    g_spatial_out = rows_product(mixed_s, grad_ys)
    g_spatial_bias = jnp.sum(grad_ys.astype(jnp.float32), 0)
    grad_mixed_s = back_product(grad_ys, spatial_out).astype(jnp.bfloat16).reshape(head_shape)
    again_s = jnp.exp(
        jnp.einsum("cfphd,cfrhd->cfhpr", query_s, key_s, preferred_element_type=jnp.float32) * 0.125
        - lse_s
    )
    grad_probs_s = jnp.einsum(
        "cfphd,cfrhd->cfhpr", grad_mixed_s, value_s, preferred_element_type=jnp.float32
    )
    grad_scores_s = softmax_back(again_s, grad_probs_s)
    grad_query_s = (
        jnp.einsum("cfhpr,cfrhd->cfphd", grad_scores_s, key_s, preferred_element_type=jnp.float32)
        * 0.125
    ).astype(jnp.bfloat16)
    grad_key_s = (
        jnp.einsum("cfhpr,cfphd->cfrhd", grad_scores_s, query_s, preferred_element_type=jnp.float32)
        * 0.125
    ).astype(jnp.bfloat16)
    grad_value_s = jnp.einsum(
        "cfhpr,cfphd->cfrhd",
        again_s.astype(jnp.bfloat16),
        grad_mixed_s,
        preferred_element_type=jnp.float32,
    ).astype(jnp.bfloat16)
    grad_packed_s = jnp.stack([grad_query_s, grad_key_s, grad_value_s], axis=3).reshape(
        row_count, 3 * model_width
    )
    g_spatial_in = rows_product(normed_s, grad_packed_s)
    time_grad, g_spatial_gain, g_spatial_shift = norm_s_back(
        back_product(grad_packed_s, spatial_in)
    )
    time_grad = space_grad + time_grad
    grad_yt = time_grad.astype(jnp.bfloat16)
    g_temporal_out = rows_product(mixed_t, grad_yt)
    g_temporal_bias = jnp.sum(grad_yt.astype(jnp.float32), 0)
    grad_mixed_flat = back_product(grad_yt, temporal_out).astype(jnp.bfloat16)
    grad_rows = lax.all_to_all(
        to_patch_rows(grad_mixed_flat, slot_count, local_frames, patch_count),
        "frame",
        split_axis=0,
        concat_axis=1,
        tiled=True,
    )
    grad_mixed_x = grad_rows.reshape(split_shape)
    again_x = jnp.exp(
        jnp.einsum("rfhd,rghd->rhfg", query_x, key_x, preferred_element_type=jnp.float32) * 0.125
        - lse_x
    )
    grad_probs_x = jnp.einsum(
        "rfhd,rghd->rhfg", grad_mixed_x, value_x, preferred_element_type=jnp.float32
    )
    grad_scores_x = softmax_back(again_x, grad_probs_x)
    grad_query_x = (
        jnp.einsum("rhfg,rghd->rfhd", grad_scores_x, key_x, preferred_element_type=jnp.float32)
        * 0.125
    ).astype(jnp.bfloat16)
    grad_key_x = (
        jnp.einsum("rhfg,rfhd->rghd", grad_scores_x, query_x, preferred_element_type=jnp.float32)
        * 0.125
    ).astype(jnp.bfloat16)
    grad_value_x = jnp.einsum(
        "rhfg,rfhd->rghd",
        again_x.astype(jnp.bfloat16),
        grad_mixed_x,
        preferred_element_type=jnp.float32,
    ).astype(jnp.bfloat16)
    packed_width = (row_part, all_frames, model_width)
    grad_stacked = jnp.concatenate(
        [
            grad_query_x.reshape(packed_width),
            grad_key_x.reshape(packed_width),
            grad_value_x.reshape(packed_width),
        ],
        axis=2,
    )
    grad_back = lax.all_to_all(grad_stacked, "frame", split_axis=1, concat_axis=0, tiled=True)
    grad_packed_t = from_patch_rows(grad_back, slot_count, local_frames, patch_count)
    g_temporal_in = rows_product(normed_t, grad_packed_t)
    input_grad, g_temporal_gain, g_temporal_shift = norm_t_back(
        back_product(grad_packed_t, temporal_in)
    )
    input_grad = time_grad + input_grad
    grads = (
        g_temporal_gain,
        g_temporal_shift,
        g_temporal_in,
        g_temporal_out,
        g_temporal_bias,
        g_spatial_gain,
        g_spatial_shift,
        g_spatial_in,
        g_spatial_out,
        g_spatial_bias,
        g_mlp_gain,
        g_mlp_shift,
        g_expand_weight,
        g_expand_bias,
        g_shrink_weight,
        g_shrink_bias,
    )
    return (
        block_rows.astype(jnp.bfloat16).reshape(tokens.shape),
        input_grad.astype(jnp.bfloat16).reshape(tokens.shape),
        grads,
    )


def generic_body(
    patch_tokens,
    live_slots,
    out_grad,
    temporal_gain,
    temporal_shift,
    temporal_in,
    temporal_out,
    temporal_bias,
    spatial_gain,
    spatial_shift,
    spatial_in,
    spatial_out,
    spatial_bias,
    mlp_gain,
    mlp_shift,
    expand_weight,
    expand_bias,
    shrink_weight,
    shrink_bias,
):
    shards = (
        temporal_gain,
        temporal_shift,
        temporal_in,
        temporal_out,
        temporal_bias,
        spatial_gain,
        spatial_shift,
        spatial_in,
        spatial_out,
        spatial_bias,
        mlp_gain,
        mlp_shift,
        expand_weight,
        expand_bias,
        shrink_weight,
        shrink_bias,
    )
    devices = lax.axis_size("clip") * lax.axis_size("frame")
    start = tuple(
        (
            jnp.zeros((member.shape[0] * devices,) + member.shape[1:], jnp.float32)
            for member in shards
        )
    )

    def one_step(totals, inputs):
        tokens, out_cot, count = inputs
        weights = (
            lax.all_gather(temporal_gain, ("clip", "frame"), axis=0, tiled=True),
            lax.all_gather(temporal_shift, ("clip", "frame"), axis=0, tiled=True),
            lax.all_gather(temporal_in, ("clip", "frame"), axis=0, tiled=True),
            lax.all_gather(temporal_out, ("clip", "frame"), axis=0, tiled=True),
            lax.all_gather(temporal_bias, ("clip", "frame"), axis=0, tiled=True),
            lax.all_gather(spatial_gain, ("clip", "frame"), axis=0, tiled=True),
            lax.all_gather(spatial_shift, ("clip", "frame"), axis=0, tiled=True),
            lax.all_gather(spatial_in, ("clip", "frame"), axis=0, tiled=True),
            lax.all_gather(spatial_out, ("clip", "frame"), axis=0, tiled=True),
            lax.all_gather(spatial_bias, ("clip", "frame"), axis=0, tiled=True),
            lax.all_gather(mlp_gain, ("clip", "frame"), axis=0, tiled=True),
            lax.all_gather(mlp_shift, ("clip", "frame"), axis=0, tiled=True),
            lax.all_gather(expand_weight, ("clip", "frame"), axis=0, tiled=True),
            lax.all_gather(expand_bias, ("clip", "frame"), axis=0, tiled=True),
            lax.all_gather(shrink_weight, ("clip", "frame"), axis=0, tiled=True),
            lax.all_gather(shrink_bias, ("clip", "frame"), axis=0, tiled=True),
        )
        block_part, grad_part, grads = micro_batch(weights, tokens, out_cot, count)
        totals = tuple((summed + addend for summed, addend in zip(totals, grads)))
        return (totals, (block_part, grad_part))

    totals, outputs = lax.scan(one_step, start, (patch_tokens, out_grad, live_slots[:, 0]))
    block_out, patch_grad = outputs
    totals = (
        lax.psum_scatter(totals[0], ("clip", "frame"), scatter_dimension=0, tiled=True),
        lax.psum_scatter(totals[1], ("clip", "frame"), scatter_dimension=0, tiled=True),
        lax.psum_scatter(totals[2], ("clip", "frame"), scatter_dimension=0, tiled=True),
        lax.psum_scatter(totals[3], ("clip", "frame"), scatter_dimension=0, tiled=True),
        lax.psum_scatter(totals[4], ("clip", "frame"), scatter_dimension=0, tiled=True),
        lax.psum_scatter(totals[5], ("clip", "frame"), scatter_dimension=0, tiled=True),
        lax.psum_scatter(totals[6], ("clip", "frame"), scatter_dimension=0, tiled=True),
        lax.psum_scatter(totals[7], ("clip", "frame"), scatter_dimension=0, tiled=True),
        lax.psum_scatter(totals[8], ("clip", "frame"), scatter_dimension=0, tiled=True),
        lax.psum_scatter(totals[9], ("clip", "frame"), scatter_dimension=0, tiled=True),
        lax.psum_scatter(totals[10], ("clip", "frame"), scatter_dimension=0, tiled=True),
        lax.psum_scatter(totals[11], ("clip", "frame"), scatter_dimension=0, tiled=True),
        lax.psum_scatter(totals[12], ("clip", "frame"), scatter_dimension=0, tiled=True),
        lax.psum_scatter(totals[13], ("clip", "frame"), scatter_dimension=0, tiled=True),
        lax.psum_scatter(totals[14], ("clip", "frame"), scatter_dimension=0, tiled=True),
        lax.psum_scatter(totals[15], ("clip", "frame"), scatter_dimension=0, tiled=True),
    )
    return (block_out, patch_grad) + tuple(totals)


def nn(left, right):
    return lax.dot_general(left, right, (((1,), (0,)), ((), ())), preferred_element_type=f32)


def nt(left, right):
    return lax.dot_general(left, right, (((1,), (1,)), ((), ())), preferred_element_type=f32)


def tn(left, right):
    return lax.dot_general(left, right, (((0,), (0,)), ((), ())), preferred_element_type=f32)


TAIL_POLE = 0.275
TAIL = (0.11782574, 0.04201021, 0.33417963, -0.33129375, 0.45218007, -0.1149019)


def gelu_parts(u):
    bell = jnp.exp(u * u * -0.5)
    t = 1.0 / (1.0 + TAIL_POLE * jnp.abs(u))
    poly = jnp.full_like(t, TAIL[5])
    for term in TAIL[4::-1]:
        poly = poly * t + term
    tail = poly * t * bell
    cdf = jnp.where(u >= 0, 1.0 - tail, tail)
    return u * cdf, cdf + u * (bell * 0.3989422804014327)


def norm_parts(v):
    centre = v - jnp.mean(v, -1, keepdims=True)
    r = lax.rsqrt(jnp.mean(centre * centre, -1, keepdims=True) + 1e-06)
    return centre * r, r


def norm_back(a, n, r, gain):
    scaled = a * gain
    return r * (
        scaled
        - jnp.mean(scaled, -1, keepdims=True)
        - n * jnp.mean(scaled * n, -1, keepdims=True)
    )


def column_sum(values):
    return jnp.sum(values, 0, keepdims=True)


def halves(pair):
    lane = lax.broadcasted_iota(jnp.int32, pair.shape, 1)
    zero = jnp.zeros_like(pair)
    return jnp.where(lane < DH, pair, zero), jnp.where(lane < DH, zero, pair)


def stacked(pair):
    return jnp.concatenate(halves(pair), axis=0)


T_GAIN, T_SHIFT, T_BIAS, S_GAIN, S_SHIFT, S_BIAS, M_GAIN, M_SHIFT, M_BIAS, HIDDEN = range(10)


def row_of(ref, at):
    return ref[at : at + 1, :]


def lanes(start, size):
    return pl.ds(pl.multiple_of(start, size), size)


def temporal_forward_kernel(
    slot_ref, own_ref, other_ref, vec_ref, win_ref,
    packed_ref, probs_ref, mixed_own_ref, mixed_other_ref, pad_s,
):
    pad_s[...] = jnp.zeros_like(pad_s)
    gain, shift = row_of(vec_ref, T_GAIN), row_of(vec_ref, T_SHIFT)
    for half, tokens_ref in enumerate((own_ref, other_ref)):

        def project(i, carry, half=half, tokens_ref=tokens_ref):
            for f in range(PAIR):
                pad_s[f, :PATCHES] = tokens_ref[PAIR * i + f]
            n, _ = norm_parts(pad_s[...].reshape(TILE, D).astype(f32))
            normed = (n * gain + shift).astype(bf16)
            at = pl.ds(half * 4 + PAIR * i, PAIR)
            packed_ref[at] = nn(normed, win_ref[...]).astype(bf16).reshape(PAIR, ROWS, 3 * D)
            return carry

        lax.fori_loop(0, 4 // PAIR, project, 0)

    row = lax.broadcasted_iota(jnp.int32, (8 * BLOCK, 8 * BLOCK), 0) % BLOCK
    col = lax.broadcasted_iota(jnp.int32, (8 * BLOCK, 8 * BLOCK), 1) % BLOCK
    same = row == col

    def attend(b, carry):
        at = pl.ds(pl.multiple_of(b * BLOCK, BLOCK), BLOCK)
        def part(h, k):
            lo = k * D + 128 * h
            return packed_ref[:, at, lo : lo + 128].reshape(8 * BLOCK, 128)

        scores, both = [], []
        for h in range(H // 2):
            query = part(h, 0) * jnp.asarray(0.125, bf16)
            scores.append(nt(query, stacked(part(h, 1))))
        for h in range(H // 2):
            probs = []
            for k in range(2):
                s = jnp.where(same, scores[h][:, 128 * k : 128 * k + 128], -1e30)
                e = jnp.exp(s - jnp.max(s, -1, keepdims=True))
                probs.append(e * (1.0 / jnp.sum(e, -1, keepdims=True)))
            both.append(jnp.concatenate(probs, axis=1).astype(bf16))
            probs_ref[b, h] = both[h]
        for h in range(H // 2):
            mixed = nn(both[h], stacked(part(h, 2))).astype(bf16).reshape(8, BLOCK, 128)
            mixed_own_ref[:, at, 128 * h : 128 * h + 128] = mixed[:4]
            mixed_other_ref[:, at, 128 * h : 128 * h + 128] = mixed[4:]
        return carry

    lax.fori_loop(0, BLOCKS, attend, 0)


def fixed(shape, at=None):
    at = at or (0,) * len(shape)
    return pl.BlockSpec(shape, lambda *ids: at, pipeline_mode=pl.Buffered(1))


def out_of(shape, kind):
    return jax.ShapeDtypeStruct(shape, kind)


def temporal_forward(slot, tokens, other, vec, weights):
    mbs = tokens.shape[0]
    frames = tokens.shape[2]
    own = pl.BlockSpec((None, None, frames, PATCHES, D), lambda m, s: (m, s[0], 0, 0, 0))
    mixed = pl.BlockSpec((None, frames, ROWS, D), lambda m, s: (m, 0, 0, 0))
    return pl.pallas_call(
        temporal_forward_kernel,
        grid_spec=pltpu.PrefetchScalarGridSpec(
            num_scalar_prefetch=1,
            grid=(mbs,),
            in_specs=[
                own,
                pl.BlockSpec((None, frames, PATCHES, D), lambda m, s: (m, 0, 0, 0)),
                fixed((16, D)),
                fixed((D, 3 * D)),
            ],
            out_specs=[
                pl.BlockSpec((None, 8, ROWS, 3 * D), lambda m, s: (m, 0, 0, 0)),
                pl.BlockSpec((None, BLOCKS, H // 2, 128, 256), lambda m, s: (m, 0, 0, 0, 0)),
                mixed,
                mixed,
            ],
            scratch_shapes=[pltpu.VMEM((PAIR, ROWS, D), bf16)],
        ),
        out_shape=[
            out_of((mbs, 8, ROWS, 3 * D), bf16),
            out_of((mbs, BLOCKS, H // 2, 128, 256), bf16),
            out_of((mbs, frames, ROWS, D), bf16),
            out_of((mbs, frames, ROWS, D), bf16),
        ],
        compiler_params=pltpu.CompilerParams(vmem_limit_bytes=VMEM_BYTES),
        cost_estimate=pl.CostEstimate(
            flops=2 * mbs * 8 * ROWS * D * 4 * D, bytes_accessed=60 << 20, transcendentals=0
        ),
        name="temporal_forward",
    )(slot, tokens, other, vec, weights)


def spatial_forward_kernel(*refs):
    slot_ref, tokens_ref, mixed_ref, vec_ref, tout_ref, sin_ref, sout_ref = refs[:7]
    time_ref, packed_ref, probs_ref, mixs_ref, space_ref, pad_s = refs[-6:]
    pad_s[...] = jnp.zeros_like(pad_s)
    for f in range(PAIR):
        pad_s[f, :PATCHES] = tokens_ref[f]
    tokens = pad_s[...].reshape(TILE, D).astype(f32)
    time = tokens + nn(mixed_ref[...].reshape(TILE, D), tout_ref[...]) + row_of(vec_ref, T_BIAS)
    time_ref[...] = time.reshape(PAIR, ROWS, D)
    n, _ = norm_parts(time)
    normed = (n * row_of(vec_ref, S_GAIN) + row_of(vec_ref, S_SHIFT)).astype(bf16)
    packed_ref[...] = nn(normed, sin_ref[...]).astype(bf16).reshape(PAIR, ROWS, 3 * D)
    valid = lax.broadcasted_iota(jnp.int32, (ROWS, ROWS), 1) < PATCHES

    def attend(g, carry):
        both = [(f, GROUP * g + i) for i in range(GROUP) for f in range(PAIR)]

        def part(f, h, k):
            return packed_ref[f, :, lanes(k * D + 128 * h, 128)]

        scores, probs = [], []
        for f, h in both:
            query = part(f, h, 0) * jnp.asarray(0.125, bf16)
            scores += [nt(query, keys) for keys in halves(part(f, h, 1))]
        for i, s in enumerate(scores):
            f, h = both[i // 2]
            s = jnp.where(valid, s, -1e30)
            e = jnp.exp(s - jnp.max(s, -1, keepdims=True))
            probs.append((e * (1.0 / jnp.sum(e, -1, keepdims=True))).astype(bf16))
            probs_ref[f, 2 * h + i % 2] = probs[i]
        for i, (f, h) in enumerate(both):
            low, high = halves(part(f, h, 2))
            total = nn(probs[2 * i], low) + nn(probs[2 * i + 1], high)
            mixs_ref[f, :, lanes(128 * h, 128)] = total.astype(bf16)
        return carry

    lax.fori_loop(0, H // 2 // GROUP, attend, 0)
    mixed = mixs_ref[...].reshape(TILE, D)
    space_ref[...] = (
        time_ref[...].reshape(TILE, D) + nn(mixed, sout_ref[...]) + row_of(vec_ref, S_BIAS)
    ).reshape(PAIR, ROWS, D)


def spatial_forward(which, slot, tokens, mixed, vec, second, earlier):
    mbs, slots, frames = tokens.shape[:3]

    def framed(*tail):
        return pl.BlockSpec(
            (None, None, PAIR) + tail, lambda m, i, s: (which, m, i) + (0,) * len(tail)
        )

    def whole(*tail):
        return (slots, mbs, frames) + tail

    shapes = [
        out_of(whole(ROWS, D), f32),
        out_of(whole(ROWS, 3 * D), bf16),
        out_of(whole(H, ROWS, ROWS), bf16),
        out_of(whole(ROWS, D), bf16),
        out_of(whole(ROWS, D), f32),
    ]
    return pl.pallas_call(
        spatial_forward_kernel,
        grid_spec=pltpu.PrefetchScalarGridSpec(
            num_scalar_prefetch=1,
            grid=(mbs, frames // PAIR),
            in_specs=[
                pl.BlockSpec(
                    (None, None, PAIR, PATCHES, D), lambda m, i, s: (m, s[which], i, 0, 0)
                ),
                pl.BlockSpec((None, PAIR, ROWS, D), lambda m, i, s: (m, i, 0, 0)),
                fixed((16, D)),
                fixed((D, D), (0, 3)),
                fixed((D, 3 * D)),
                fixed((D, D), (0, 4)),
            ]
            + [pl.BlockSpec(memory_space=pl.ANY)] * len(earlier),
            out_specs=[
                framed(ROWS, D),
                framed(ROWS, 3 * D),
                framed(H, ROWS, ROWS),
                framed(ROWS, D),
                framed(ROWS, D),
            ],
            scratch_shapes=[pltpu.VMEM((PAIR, ROWS, D), bf16)],
        ),
        out_shape=shapes,
        input_output_aliases={7 + i: i for i in range(len(earlier))},
        compiler_params=pltpu.CompilerParams(vmem_limit_bytes=VMEM_BYTES),
        cost_estimate=pl.CostEstimate(
            flops=2 * mbs * frames * ROWS * D * 6 * D, bytes_accessed=60 << 20, transcendentals=0
        ),
        name="spatial_forward",
    )(slot, tokens, mixed, vec, second, second, second, *earlier)


def mlp_kernel(
    slot_ref, live_ref, space_ref, cotan_ref, vec_ref, hidden_ref, expand_ref, shrink_ref,
    out_ref, grad_ref, weights_ref, sums_ref, hidden_sums_ref,
    z_s, normed_s, total_s, back_s, expand_s, shrink_s,
):
    i = pl.program_id(0)

    @pl.when(i == 0)
    def _():
        expand_s[...] = jnp.zeros_like(expand_s)
        shrink_s[...] = jnp.zeros_like(shrink_s)
        sums_ref[...] = jnp.zeros_like(sums_ref)
        hidden_sums_ref[...] = jnp.zeros_like(hidden_sums_ref)
        z_s[...] = jnp.zeros_like(z_s)

    gain = row_of(vec_ref, M_GAIN)
    live = live_ref[i]
    for f in range(PAIR):
        cotan = cotan_ref[f]
        z_s[f, :PATCHES] = jnp.where(live > 0, cotan, jnp.zeros_like(cotan))
    grad_z = z_s[...].reshape(TILE, D)
    space = space_ref[...].reshape(TILE, D)
    n, _ = norm_parts(space)
    normed = (n * gain + row_of(vec_ref, M_SHIFT)).astype(bf16)
    normed_s[...] = normed
    total_s[...] = space + row_of(vec_ref, M_BIAS)
    back_s[...] = jnp.zeros_like(back_s)
    normed_turned = normed.T
    z_turned = grad_z.T

    def ahead(j):
        at = slice(j * CHUNK, (j + 1) * CHUNK)
        hidden = nn(normed_s[...], expand_ref[:, at]) + hidden_ref[:, at]
        return hidden, nt(grad_z, shrink_ref[:, at])

    pending = ahead(0)
    for j in range(CHUNKS):
        at = slice(j * CHUNK, (j + 1) * CHUNK)
        hidden, grad_active = pending
        if j + 1 < CHUNKS:
            pending = ahead(j + 1)
        active, slope = gelu_parts(hidden)
        active = active.astype(bf16)
        grad_hidden = (slope * grad_active).astype(bf16)
        total_s[...] += nn(active, shrink_ref[:, at])
        shrink_s[:, at] += nn(z_turned, active)
        expand_s[:, at] += nn(normed_turned, grad_hidden)
        back_s[...] += nt(grad_hidden, expand_ref[:, at])
        hidden_sums_ref[0:1, at] += column_sum(grad_hidden.astype(f32))
    block_out = total_s[...].reshape(PAIR, ROWS, D)
    for f in range(PAIR):
        out_ref[f] = block_out[f, :PATCHES].astype(bf16)
    a = back_s[...]
    n, r = norm_parts(space_ref[...].reshape(TILE, D))
    wide_z = grad_z.astype(f32)
    grad_ref[...] = (wide_z + norm_back(a, n, r, gain)).reshape(PAIR, ROWS, D)
    sums_ref[0:1] += column_sum(a * n)
    sums_ref[1:2] += column_sum(a)
    sums_ref[2:3] += column_sum(wide_z)

    @pl.when(i == pl.num_programs(0) - 1)
    def _():
        weights_ref[:, : CHUNKS * CHUNK] = expand_s[...].astype(bf16)
        for j in range(CHUNKS):
            lo = j * CHUNK
            weights_ref[:, CHUNKS * CHUNK + lo : CHUNKS * CHUNK + lo + D] = (
                shrink_s[:, lo : lo + CHUNK].T.astype(bf16)
            )


def mlp(slot, live, space, cotan, vec, hidden, third):
    slots, mbs, frames = space.shape[:3]
    per = frames // PAIR
    steps = slots * mbs * per

    def placed(i):
        return i // (mbs * per), (i // per) % mbs, i % per

    def by_slot(i, s, live):
        r, m, f = placed(i)
        return m, s[r], f, 0, 0

    def framed(i, s, live):
        return placed(i) + (0, 0)

    outer = pl.BlockSpec((None, None, PAIR, PATCHES, D), by_slot)
    inner = pl.BlockSpec((None, None, PAIR, ROWS, D), framed)
    width = CHUNKS * CHUNK
    return pl.pallas_call(
        mlp_kernel,
        grid_spec=pltpu.PrefetchScalarGridSpec(
            num_scalar_prefetch=2,
            grid=(steps,),
            in_specs=[
                inner,
                outer,
                fixed((16, D)),
                fixed((1, width)),
                fixed((D, width), (0, 0)),
                fixed((D, width), (0, 1)),
            ],
            out_specs=[
                outer,
                inner,
                fixed((D, 2 * width)),
                fixed((8, D)),
                fixed((8, width)),
            ],
            scratch_shapes=[
                pltpu.VMEM((PAIR, ROWS, D), bf16),
                pltpu.VMEM((TILE, D), bf16),
                pltpu.VMEM((TILE, D), f32),
                pltpu.VMEM((TILE, D), f32),
                pltpu.VMEM((D, width), f32),
                pltpu.VMEM((D, width), f32),
            ],
        ),
        out_shape=[
            out_of(cotan.shape, bf16),
            out_of(space.shape, f32),
            out_of((D, 2 * width), bf16),
            out_of((8, D), f32),
            out_of((8, width), f32),
        ],
        compiler_params=pltpu.CompilerParams(vmem_limit_bytes=VMEM_BYTES),
        cost_estimate=pl.CostEstimate(
            flops=12 * steps * TILE * D * width, bytes_accessed=60 << 20, transcendentals=0
        ),
        name="mlp",
    )(slot, live, space, cotan, vec, hidden, third, third)


def spatial_backward_kernel(first_call, *refs):
    (
        grad_ref, packed_ref, probs_ref, mixs_ref, time_ref, mixed_ref,
        vec_ref, tout_ref, sin_ref, sout_ref,
    ) = refs[:10]
    if first_call:
        weights_ref, sums_ref, time_grad_ref, back_ref, gmix_s, gpack_s = refs[-6:]
        in_acc = out_acc = tail_acc = None
        total = weights_ref
    else:
        total_ref, sums_before_ref = refs[10:12]
        weights_ref, sums_ref, time_grad_ref, back_ref, gmix_s, gpack_s, total = refs[-7:]
    step = pl.program_id(0) * pl.num_programs(1) + pl.program_id(1)
    steps = pl.num_programs(0) * pl.num_programs(1)

    @pl.when(step == 0)
    def _():
        if first_call:
            total[...] = jnp.zeros_like(total)
            sums_ref[...] = jnp.zeros_like(sums_ref)
        else:
            pltpu.sync_copy(total_ref, total)
            sums_ref[...] = sums_before_ref[...]

    gain = row_of(vec_ref, S_GAIN)
    space_grad = grad_ref[...].reshape(TILE, D)
    grad_ys = space_grad.astype(bf16)
    total[:, 3 * D : 4 * D] += tn(mixs_ref[...].reshape(TILE, D), grad_ys)
    gmix_s[...] = nt(grad_ys, sout_ref[...]).astype(bf16).reshape(PAIR, ROWS, D)

    def attend(g, carry):
        both = [(f, GROUP * g + i) for i in range(GROUP) for f in range(PAIR)]

        def part(f, h, k):
            return packed_ref[f, :, lanes(k * D + 128 * h, 128)]

        products, scores = [], []
        for f, h in both:
            out_pair = gmix_s[f, :, lanes(128 * h, 128)]
            products += [nt(out_pair, values) for values in halves(part(f, h, 2))]
        for i, product in enumerate(products):
            f, h = both[i // 2]
            wide = probs_ref[f, 2 * h + i % 2].astype(f32)
            product = wide * product
            scores.append(
                (product - wide * jnp.sum(product, -1, keepdims=True)).astype(bf16)
            )
        for i, (f, h) in enumerate(both):
            outs = halves(gmix_s[f, :, lanes(128 * h, 128)])
            queries, keys = halves(part(f, h, 0)), halves(part(f, h, 1))
            near = scores[2 * i : 2 * i + 2]
            grad_v = tn(probs_ref[f, 2 * h], outs[0]) + tn(probs_ref[f, 2 * h + 1], outs[1])
            grad_q = nn(near[0], keys[0]) + nn(near[1], keys[1])
            grad_k = tn(near[0], queries[0]) + tn(near[1], queries[1])
            gpack_s[f, :, lanes(128 * h, 128)] = (grad_q * 0.125).astype(bf16)
            gpack_s[f, :, lanes(D + 128 * h, 128)] = (grad_k * 0.125).astype(bf16)
            gpack_s[f, :, lanes(2 * D + 128 * h, 128)] = grad_v.astype(bf16)
        return carry

    lax.fori_loop(0, H // 2 // GROUP, attend, 0)
    n, r = norm_parts(time_ref[...].reshape(TILE, D))
    normed = (n * gain + row_of(vec_ref, S_SHIFT)).astype(bf16)
    grad_packed = gpack_s[...].reshape(TILE, 3 * D)
    total[:, : 3 * D] += tn(normed, grad_packed)
    a = nt(grad_packed, sin_ref[...])
    time_grad = grad_ref[...].reshape(TILE, D) + norm_back(a, n, r, gain)
    time_grad_ref[...] = time_grad.reshape(PAIR, ROWS, D)
    grad_yt = time_grad.astype(bf16)
    total[:, 4 * D :] += tn(mixed_ref[...].reshape(TILE, D), grad_yt)
    back_ref[...] = nt(grad_yt, tout_ref[...]).astype(bf16).reshape(PAIR, ROWS, D)
    sums_ref[0:1] += column_sum(a * n)
    sums_ref[1:2] += column_sum(a)
    sums_ref[2:3] += column_sum(grad_ys.astype(f32))
    sums_ref[3:4] += column_sum(grad_yt.astype(f32))
    if not first_call:

        @pl.when(step == steps - 1)
        def _():
            weights_ref[...] = total[...].astype(bf16)


def spatial_backward(which, grad, packed, probs, mixs, time, mixed, vec, second, earlier):
    slots, mbs, frames = grad.shape[:3]

    def framed(*tail):
        return pl.BlockSpec(
            (None, None, PAIR) + tail, lambda m, i: (which, m, i) + (0,) * len(tail)
        )

    single = pl.BlockSpec((None, PAIR, ROWS, D), lambda m, i: (m, i, 0, 0))
    scratch = [pltpu.VMEM((PAIR, ROWS, D), bf16), pltpu.VMEM((PAIR, ROWS, 3 * D), bf16)]
    extra = []
    if earlier:
        extra = [pl.BlockSpec(memory_space=pl.ANY), fixed((8, D))]
        scratch = scratch + [pltpu.VMEM((D, 5 * D), f32)]

    def kernel(*refs):
        return spatial_backward_kernel(not earlier, *refs)

    return pl.pallas_call(
        kernel,
        grid=(mbs, frames // PAIR),
        in_specs=[
            framed(ROWS, D),
            framed(ROWS, 3 * D),
            framed(H, ROWS, ROWS),
            framed(ROWS, D),
            framed(ROWS, D),
            single,
            fixed((16, D)),
            fixed((D, D), (0, 3)),
            fixed((D, 3 * D)),
            fixed((D, D), (0, 4)),
        ]
        + extra,
        out_specs=[fixed((D, 5 * D)), fixed((8, D)), single, single],
        out_shape=[
            out_of((D, 5 * D), bf16 if earlier else f32),
            out_of((8, D), f32),
            out_of((mbs, frames, ROWS, D), f32),
            out_of((mbs, frames, ROWS, D), bf16),
        ],
        scratch_shapes=scratch,
        compiler_params=pltpu.CompilerParams(vmem_limit_bytes=VMEM_BYTES),
        cost_estimate=pl.CostEstimate(
            flops=2 * mbs * frames * ROWS * D * 14 * D, bytes_accessed=60 << 20, transcendentals=0
        ),
        name="spatial_backward",
    )(grad, packed, probs, mixs, time, mixed, vec, second, second, second, *earlier)


def temporal_backward_kernel(
    slot_ref, own_ref, other_ref, packed_ref, probs_ref, back_own_ref, back_other_ref,
    vec_ref, win_ref, space_sums_ref, mlp_sums_ref, hidden_sums_ref, space_ref,
    weights_ref, gpack_ref, pad_s, total_s, sums_s, columns_s, copied,
):
    m, j = pl.program_id(0), pl.program_id(1)
    taken = pltpu.make_async_copy(space_ref, weights_ref.at[:, 3 * D + 128 :], copied)

    @pl.when((m == 0) & (j == 0))
    def _():
        taken.start()
        total_s[...] = jnp.zeros_like(total_s)
        columns_s[...] = jnp.zeros_like(columns_s)
        sums_s[...] = jnp.zeros_like(sums_s)
        sums_s[T_BIAS : T_BIAS + 1] = space_sums_ref[3:4]
        sums_s[S_GAIN : S_GAIN + 3] = space_sums_ref[0:3]
        sums_s[M_GAIN : M_GAIN + 3] = mlp_sums_ref[0:3]
        for k in range(CHUNKS):
            sums_s[HIDDEN + k : HIDDEN + k + 1] = hidden_sums_ref[0:1, k * D : (k + 1) * D]
        sums_s[16:32] = vec_ref[...]
        pad_s[...] = jnp.zeros_like(pad_s)

    @pl.when(j < BLOCKS)
    def _():
        at = pl.ds(pl.multiple_of(jnp.minimum(j, BLOCKS - 1) * BLOCK, BLOCK), BLOCK)

        def part(h, k):
            lo = k * D + 128 * h
            return packed_ref[:, :, lo : lo + 128].reshape(8 * BLOCK, 128)

        def out_pair(h):
            lo = 128 * h
            return jnp.concatenate(
                [back_own_ref[:, :, lo : lo + 128], back_other_ref[:, :, lo : lo + 128]], axis=0
            ).reshape(8 * BLOCK, 128)

        products = [nt(out_pair(h), stacked(part(h, 2))) for h in range(H // 2)]
        scores = []
        for h in range(H // 2):
            wide = probs_ref[h].astype(f32)
            product = wide * products[h]
            pair = []
            for k in range(2):
                near = product[:, 128 * k : 128 * k + 128]
                weight = wide[:, 128 * k : 128 * k + 128]
                pair.append((near - weight * jnp.sum(near, -1, keepdims=True)).astype(bf16))
            scores.append(pair)
        for h in range(H // 2):
            lo = 128 * h
            probs = probs_ref[h]
            grad_v = tn(
                jnp.concatenate([probs[:, :128], probs[:, 128:]], axis=0), stacked(out_pair(h))
            )
            grad_q = nn(jnp.concatenate(scores[h], axis=1), stacked(part(h, 1))) * 0.125
            grad_k = tn(jnp.concatenate(scores[h], axis=0), stacked(part(h, 0))) * 0.125
            for k, values_of in enumerate((grad_q, grad_k, grad_v)):
                gpack_ref[:, at, k * D + lo : k * D + lo + 128] = values_of.astype(bf16).reshape(
                    8, BLOCK, 128
                )

    @pl.when(j >= BLOCKS)
    def _():
        p = jnp.clip(j - BLOCKS, 0, 1)
        for f in range(HALF):
            pad_s[f, :PATCHES] = jnp.where(p == 0, own_ref[f], other_ref[f])
        n, _ = norm_parts(pad_s[...].reshape(HALF * ROWS, D).astype(f32))
        grad_packed = gpack_ref[pl.ds(HALF * p, HALF)].reshape(HALF * ROWS, 3 * D)
        total_s[...] += tn(n.astype(bf16), grad_packed)
        columns_s[0:1] += column_sum(grad_packed.astype(f32))

    @pl.when((m == pl.num_programs(0) - 1) & (j == pl.num_programs(1) - 1))
    def _():
        taken.wait()
        turned = sums_s[...].T
        gain, shift = turned[:, 16 + T_GAIN : 17 + T_GAIN], turned[:, 16 + T_SHIFT : 17 + T_SHIFT]
        g_gain = jnp.zeros((D, 1), f32)
        g_shift = jnp.zeros((D, 1), f32)
        for k in range(3):
            at = slice(k * D, (k + 1) * D)
            total, columns = total_s[:, at], columns_s[0:1, at]
            win = win_ref[:, at].astype(f32)
            weights_ref[:, at] = (gain * total + shift * columns).astype(bf16)
            g_gain = g_gain + jnp.sum(total * win, -1, keepdims=True)
            g_shift = g_shift + jnp.sum(columns * win, -1, keepdims=True)
        lane = lax.broadcasted_iota(jnp.int32, (D, 128), 1)
        turned = jnp.where(lane == T_GAIN, g_gain, jnp.where(lane == T_SHIFT, g_shift, turned))
        weights_ref[:, 3 * D : 3 * D + 128] = turned.astype(bf16)


def temporal_backward(
    slot, tokens, other, packed, probs, back_own, back_other, vec, weights,
    space_sums, mlp_sums, hidden_sums, space,
):
    mbs, slots, frames = tokens.shape[:3]
    def row_block(j):
        return jnp.minimum(j, BLOCKS - 1)

    rows_of = pl.BlockSpec((None, frames, BLOCK, D), lambda m, j, s: (m, 0, row_block(j), 0))
    return pl.pallas_call(
        temporal_backward_kernel,
        grid_spec=pltpu.PrefetchScalarGridSpec(
            num_scalar_prefetch=1,
            grid=(mbs, BLOCKS + 2),
            in_specs=[
                pl.BlockSpec((None, None, HALF, PATCHES, D), lambda m, j, s: (m, s[0], 0, 0, 0)),
                pl.BlockSpec((None, HALF, PATCHES, D), lambda m, j, s: (m, 0, 0, 0)),
                pl.BlockSpec((None, 8, BLOCK, 3 * D), lambda m, j, s: (m, 0, row_block(j), 0)),
                pl.BlockSpec(
                    (None, None, H // 2, 128, 256), lambda m, j, s: (m, row_block(j), 0, 0, 0)
                ),
                rows_of,
                rows_of,
                fixed((16, D)),
                fixed((D, 3 * D)),
                fixed((8, D)),
                fixed((8, D)),
                fixed((8, CHUNKS * D)),
                pl.BlockSpec(memory_space=pl.ANY),
            ],
            out_specs=[
                fixed((D, 8 * D + 128)),
                pl.BlockSpec((None, 8, ROWS, 3 * D), lambda m, j, s: (m, 0, 0, 0)),
            ],
            scratch_shapes=[
                pltpu.VMEM((HALF, ROWS, D), bf16),
                pltpu.VMEM((D, 3 * D), f32),
                pltpu.VMEM((128, D), f32),
                pltpu.VMEM((8, 3 * D), f32),
                pltpu.SemaphoreType.DMA(()),
            ],
        ),
        out_shape=[
            out_of((D, 8 * D + 128), bf16),
            out_of((mbs, 8, ROWS, 3 * D), bf16),
        ],
        compiler_params=pltpu.CompilerParams(vmem_limit_bytes=VMEM_BYTES),
        cost_estimate=pl.CostEstimate(
            flops=2 * mbs * 8 * ROWS * D * 5 * D, bytes_accessed=60 << 20, transcendentals=0
        ),
        name="temporal_backward",
    )(
        slot, tokens, other, packed, probs, back_own, back_other, vec, weights,
        space_sums, mlp_sums, hidden_sums, space,
    )


def input_grad_kernel(own, *refs):
    tokens_ref, gpack_ref, vec_ref, win_ref = refs[1:5]
    out_ref, pad_s = refs[-2:]
    pad_s[...] = jnp.zeros_like(pad_s)
    for f in range(PAIR):
        pad_s[f, :PATCHES] = tokens_ref[f]
    n, r = norm_parts(pad_s[...].reshape(TILE, D).astype(f32))
    a = nt(gpack_ref[...].reshape(TILE, 3 * D), win_ref[...])
    back = norm_back(a, n, r, row_of(vec_ref, T_GAIN)).reshape(PAIR, ROWS, D)
    if own:
        back = back + refs[5][...]
        for f in range(PAIR):
            out_ref[f] = back[f, :PATCHES].astype(bf16)
    else:
        out_ref[...] = back.astype(bf16)


def input_grad(own, slot, tokens, gpack, vec, weights, extra, frames):
    mbs = gpack.shape[0]
    near = frames // PAIR
    half = 0 if own else near
    single = pl.BlockSpec((None, PAIR, ROWS, D), lambda m, i, s: (m, i, 0, 0))
    outer = pl.BlockSpec((None, None, PAIR, PATCHES, D), lambda m, i, s: (m, s[0], i, 0, 0))
    other = pl.BlockSpec((None, PAIR, PATCHES, D), lambda m, i, s: (m, i, 0, 0))

    def kernel(*refs):
        input_grad_kernel(own, *refs)

    return pl.pallas_call(
        kernel,
        grid_spec=pltpu.PrefetchScalarGridSpec(
            num_scalar_prefetch=1,
            grid=(mbs, near),
            in_specs=[
                outer if own else other,
                pl.BlockSpec((None, PAIR, ROWS, 3 * D), lambda m, i, s: (m, half + i, 0, 0)),
                fixed((16, D)),
                fixed((D, 3 * D)),
            ]
            + [single] * len(extra),
            out_specs=outer if own else single,
            scratch_shapes=[pltpu.VMEM((PAIR, ROWS, D), bf16)],
        ),
        out_shape=out_of(tokens.shape if own else (mbs, frames, ROWS, D), bf16),
        compiler_params=pltpu.CompilerParams(vmem_limit_bytes=VMEM_BYTES),
        cost_estimate=pl.CostEstimate(
            flops=2 * mbs * frames * ROWS * D * 3 * D, bytes_accessed=20 << 20, transcendentals=0
        ),
        name="input_grad",
    )(slot, tokens, gpack, vec, weights, *extra)


def last_sum_kernel(slot_ref, time_grad_ref, back_ref, patch_in_ref, patch_ref):
    del patch_in_ref
    whole = time_grad_ref[...] + back_ref[...].astype(f32)
    for f in range(PAIR):
        patch_ref[f] = whole[f, :PATCHES].astype(bf16)


def last_sum(slot, time_grad, back, patch):
    mbs, frames = time_grad.shape[:2]
    single = pl.BlockSpec((None, PAIR, ROWS, D), lambda m, i, s: (m, i, 0, 0))
    return pl.pallas_call(
        last_sum_kernel,
        grid_spec=pltpu.PrefetchScalarGridSpec(
            num_scalar_prefetch=1,
            grid=(mbs, frames // PAIR),
            in_specs=[single, single, pl.BlockSpec(memory_space=pl.ANY)],
            out_specs=pl.BlockSpec(
                (None, None, PAIR, PATCHES, D), lambda m, i, s: (m, s[1], i, 0, 0)
            ),
        ),
        out_shape=out_of(patch.shape, bf16),
        input_output_aliases={3: 0},
        name="last_sum",
    )(slot, time_grad, back, patch)


AXES = ("clip", "frame")


def swap(values):
    return lax.ppermute(values, "frame", [(0, 1), (1, 0)])


def gather(values):
    return lax.all_gather(values, AXES, axis=0, tiled=True)


def scatter_sum(values):
    return lax.psum_scatter(values, AXES, scatter_dimension=0, tiled=True)


def paired_body(
    patch_tokens, live_slots, out_grad,
    temporal_gain, temporal_shift, temporal_in, temporal_out, temporal_bias,
    spatial_gain, spatial_shift, spatial_in, spatial_out, spatial_bias,
    mlp_gain, mlp_shift, expand_weight, expand_bias, shrink_weight, shrink_bias,
):
    rows = temporal_in.shape[0]
    mine = lax.axis_index("frame")
    slot = jnp.stack([mine, 1 - mine]).astype(jnp.int32)
    sent = lax.dynamic_index_in_dim(patch_tokens, 1 - mine, 1, keepdims=False)
    other = swap(sent)

    columns = [
        v[:, None]
        for v in (
            temporal_gain, temporal_shift, temporal_bias, spatial_gain, spatial_shift,
            spatial_bias, mlp_gain, mlp_shift, shrink_bias,
        )
    ] + [expand_bias.reshape(rows, CHUNKS)]
    columns = jnp.concatenate(columns, axis=1)
    columns = jnp.pad(columns, ((0, 0), (0, 128 - columns.shape[1])))
    first = gather(jnp.concatenate([temporal_in, columns], axis=1))
    second = gather(jnp.concatenate([spatial_in, temporal_out, spatial_out], axis=1))
    turned = expand_weight.reshape(rows, D, CHUNKS).transpose(0, 2, 1).reshape(rows, CHUNKS * D)
    third = gather(
        jnp.concatenate([turned, shrink_weight.reshape(rows, CHUNKS * D)], axis=1)
    )
    vec = first[:, 3 * D :].T[:16].astype(f32)
    hidden = vec[HIDDEN : HIDDEN + CHUNKS].reshape(1, CHUNKS * D)

    mbs, frames = patch_tokens.shape[0], patch_tokens.shape[2]
    packed_t, probs_t, mixed_own, mixed_other = temporal_forward(
        slot, patch_tokens, other, vec, first
    )
    mixed_here = swap(mixed_other)
    saved = spatial_forward(0, slot, patch_tokens, mixed_own, vec, second, ())
    saved = spatial_forward(1, slot, patch_tokens, mixed_here, vec, second, saved)
    time, packed_s, probs_s, mixed_s, space = saved

    live = (slot[:, None] < live_slots[:, 0][None, :]).astype(jnp.int32)
    live = jnp.repeat(live.reshape(-1), frames // PAIR)
    block_out, space_grad, g_mlp, sums_m, sums_h = mlp(
        slot, live, space, out_grad, vec, hidden, third
    )
    g_mlp = scatter_sum(g_mlp)

    kept = (space_grad, packed_s, probs_s, mixed_s, time)
    g_far, sums_s, time_grad_far, back_far = spatial_backward(
        1, *kept, mixed_here, vec, second, ()
    )
    back_other = swap(back_far)
    g_space, sums_s, time_grad_own, back_own = spatial_backward(
        0, *kept, mixed_own, vec, second, (g_far, sums_s)
    )
    g_rest, gpack = temporal_backward(
        slot, patch_tokens, other, packed_t, probs_t, back_own, back_other, vec, first,
        sums_s, sums_m, sums_h, g_space,
    )
    g_rest, g_mlp = lax.optimization_barrier((g_rest, g_mlp))
    g_rest = scatter_sum(g_rest)
    send = input_grad(False, slot, other, gpack, vec, first, (), frames)
    patch_grad = input_grad(
        True, slot, patch_tokens, gpack, vec, first, (time_grad_own,), frames
    )
    patch_grad = last_sum(slot, time_grad_far, swap(send), patch_grad)

    g_rest, g_mlp = g_rest.astype(f32), g_mlp.astype(f32)
    tail, g_space = g_rest[:, 3 * D : 3 * D + 128], g_rest[:, 3 * D + 128 :]

    def vector(at):
        return tail[:, at]

    wide = CHUNKS * D
    g_expand = g_mlp[:, :wide].reshape(rows, CHUNKS, D).transpose(0, 2, 1).reshape(rows, wide)
    return (
        block_out,
        patch_grad,
        vector(T_GAIN),
        vector(T_SHIFT),
        g_rest[:, : 3 * D],
        g_space[:, 4 * D :],
        vector(T_BIAS),
        vector(S_GAIN),
        vector(S_SHIFT),
        g_space[:, : 3 * D],
        g_space[:, 3 * D : 4 * D],
        vector(S_BIAS),
        vector(M_GAIN),
        vector(M_SHIFT),
        g_expand,
        tail[:, HIDDEN : HIDDEN + CHUNKS].reshape(rows * CHUNKS),
        g_mlp[:, wide:].reshape(rows * CHUNKS, D),
        vector(M_BIAS),
    )


def body(*args):
    tokens, temporal_in, expand_weight = args[0], args[5], args[15]
    paired = (
        lax.axis_size("frame") == 2
        and tokens.shape[1:] == (2, 4, PATCHES, D)
        and temporal_in.shape[1] == 3 * D
        and expand_weight.shape[1] == CHUNKS * CHUNK
    )
    return paired_body(*args) if paired else generic_body(*args)


def solution(mesh):
    placed = (
        P(None, "clip", "frame", None, None),
        P(None, "clip"),
        P(None, "clip", "frame", None, None),
        P(("clip", "frame")),
        P(("clip", "frame")),
        P(("clip", "frame"), None),
        P(("clip", "frame"), None),
        P(("clip", "frame")),
        P(("clip", "frame")),
        P(("clip", "frame")),
        P(("clip", "frame"), None),
        P(("clip", "frame"), None),
        P(("clip", "frame")),
        P(("clip", "frame")),
        P(("clip", "frame")),
        P(("clip", "frame"), None),
        P(("clip", "frame")),
        P(("clip", "frame"), None),
        P(("clip", "frame")),
    )
    return jax.shard_map(
        body,
        mesh=mesh,
        in_specs=placed,
        out_specs=(
            P(None, "clip", "frame", None, None),
            P(None, "clip", "frame", None, None),
            P(("clip", "frame")),
            P(("clip", "frame")),
            P(("clip", "frame"), None),
            P(("clip", "frame"), None),
            P(("clip", "frame")),
            P(("clip", "frame")),
            P(("clip", "frame")),
            P(("clip", "frame"), None),
            P(("clip", "frame"), None),
            P(("clip", "frame")),
            P(("clip", "frame")),
            P(("clip", "frame")),
            P(("clip", "frame"), None),
            P(("clip", "frame")),
            P(("clip", "frame"), None),
            P(("clip", "frame")),
        ),
        check_vma=False,
    )
```

```python
import jax
import jax.numpy as jnp
from jax import lax
from jax.experimental import pallas as pl
from jax.experimental.pallas import tpu as pltpu
from jax.sharding import PartitionSpec as P

H = 12
DH = 64
D = 768
PATCHES = 196
ROWS = 208
PAIR = 2
HALF = 4
TILE = PAIR * ROWS
GROUP = 3
BACK_GROUP = 6
CHUNK = 768
CHUNKS = 4
BLOCK = 16
BLOCKS = ROWS // BLOCK
VMEM_BYTES = 66 * 1000 * 1000
bf16 = jnp.bfloat16
f32 = jnp.float32


def layer_norm(values, gain, shift):
    centre = values - jnp.mean(values, -1, keepdims=True)
    spread = jnp.mean(centre * centre, -1, keepdims=True)
    return centre * lax.rsqrt(spread + 1e-06) * gain + shift


def exact_gelu(values):
    return jax.nn.gelu(values, approximate=False)


def rows_product(left, right):
    return lax.dot_general(
        left, right, (((0,), (0,)), ((), ())), preferred_element_type=jnp.float32
    )


def back_product(grads_in, weight):
    return lax.dot_general(
        grads_in, weight, (((1,), (1,)), ((), ())), preferred_element_type=jnp.float32
    )


def forward_dot(left, right):
    return jnp.dot(left, right, preferred_element_type=jnp.float32)


def softmax_parts(scores):
    top_value = jnp.max(scores, -1, keepdims=True)
    expo_value = jnp.exp(scores - top_value)
    total_value = jnp.sum(expo_value, -1, keepdims=True)
    return (expo_value / total_value, top_value + jnp.log(total_value))


def softmax_back(probs, grad_probs):
    return (probs * (grad_probs - jnp.sum(probs * grad_probs, -1, keepdims=True))).astype(
        jnp.bfloat16
    )


def to_patch_rows(values, slot_count, local_frames, patch_count):
    width = values.shape[-1]
    return (
        values.reshape(slot_count, local_frames, patch_count, width)
        .transpose(0, 2, 1, 3)
        .reshape(slot_count * patch_count, local_frames, width)
    )


def from_patch_rows(values, slot_count, local_frames, patch_count):
    width = values.shape[-1]
    return (
        values.reshape(slot_count, patch_count, local_frames, width)
        .transpose(0, 2, 1, 3)
        .reshape(slot_count * local_frames * patch_count, width)
    )


def micro_batch(weights, tokens, out_cot, count):
    (
        temporal_gain,
        temporal_shift,
        temporal_in,
        temporal_out,
        temporal_bias,
        spatial_gain,
        spatial_shift,
        spatial_in,
        spatial_out,
        spatial_bias,
        mlp_gain,
        mlp_shift,
        expand_weight,
        expand_bias,
        shrink_weight,
        shrink_bias,
    ) = weights
    slot_count, local_frames, patch_count, model_width = tokens.shape
    row_count = slot_count * local_frames * patch_count
    head_shape = (slot_count, local_frames, patch_count, H, DH)
    live_mask = (jnp.arange(slot_count) < count).astype(jnp.float32)[:, None, None, None]
    cotan = (out_cot.astype(jnp.float32) * live_mask).reshape(row_count, model_width)
    flat_in = tokens.astype(jnp.float32).reshape(row_count, model_width)
    normed_t, norm_t_back = jax.vjp(
        layer_norm, flat_in, temporal_gain.astype(jnp.float32), temporal_shift.astype(jnp.float32)
    )
    normed_t = normed_t.astype(jnp.bfloat16)
    packed_t = forward_dot(normed_t, temporal_in).astype(jnp.bfloat16)
    frame_rows = lax.all_to_all(
        to_patch_rows(packed_t, slot_count, local_frames, patch_count),
        "frame",
        split_axis=0,
        concat_axis=1,
        tiled=True,
    )
    row_part, all_frames = (frame_rows.shape[0], frame_rows.shape[1])
    split_shape = (row_part, all_frames, H, DH)
    query_x = frame_rows[:, :, :model_width].reshape(split_shape)
    key_x = frame_rows[:, :, model_width : 2 * model_width].reshape(split_shape)
    value_x = frame_rows[:, :, 2 * model_width :].reshape(split_shape)
    scores_x = (
        jnp.einsum("rfhd,rghd->rhfg", query_x, key_x, preferred_element_type=jnp.float32) * 0.125
    )
    probs_x, lse_x = softmax_parts(scores_x)
    mixed_x = jnp.einsum(
        "rhfg,rghd->rfhd", probs_x.astype(jnp.bfloat16), value_x, preferred_element_type=jnp.float32
    )
    mixed_x = mixed_x.astype(jnp.bfloat16).reshape(row_part, all_frames, model_width)
    mixed_back = lax.all_to_all(mixed_x, "frame", split_axis=1, concat_axis=0, tiled=True)
    mixed_t = from_patch_rows(mixed_back, slot_count, local_frames, patch_count)
    after_time = flat_in + forward_dot(mixed_t, temporal_out) + temporal_bias.astype(jnp.float32)
    normed_s, norm_s_back = jax.vjp(
        layer_norm, after_time, spatial_gain.astype(jnp.float32), spatial_shift.astype(jnp.float32)
    )
    normed_s = normed_s.astype(jnp.bfloat16)
    packed_s = (
        forward_dot(normed_s, spatial_in)
        .astype(jnp.bfloat16)
        .reshape(slot_count, local_frames, patch_count, 3, H, DH)
    )
    query_s = packed_s[:, :, :, 0]
    key_s = packed_s[:, :, :, 1]
    value_s = packed_s[:, :, :, 2]
    scores_s = (
        jnp.einsum("cfphd,cfrhd->cfhpr", query_s, key_s, preferred_element_type=jnp.float32) * 0.125
    )
    probs_s, lse_s = softmax_parts(scores_s)
    mixed_s = jnp.einsum(
        "cfhpr,cfrhd->cfphd",
        probs_s.astype(jnp.bfloat16),
        value_s,
        preferred_element_type=jnp.float32,
    )
    mixed_s = mixed_s.astype(jnp.bfloat16).reshape(row_count, model_width)
    after_space = after_time + forward_dot(mixed_s, spatial_out) + spatial_bias.astype(jnp.float32)
    normed_m, norm_m_back = jax.vjp(
        layer_norm, after_space, mlp_gain.astype(jnp.float32), mlp_shift.astype(jnp.float32)
    )
    normed_m = normed_m.astype(jnp.bfloat16)
    hidden = forward_dot(normed_m, expand_weight) + expand_bias.astype(jnp.float32)
    active, gelu_back = jax.vjp(exact_gelu, hidden)
    active = active.astype(jnp.bfloat16)
    block_rows = after_space + forward_dot(active, shrink_weight) + shrink_bias.astype(jnp.float32)
    grad_z = cotan.astype(jnp.bfloat16)
    g_shrink_weight = rows_product(active, grad_z)
    g_shrink_bias = jnp.sum(grad_z.astype(jnp.float32), 0)
    grad_hidden = gelu_back(back_product(grad_z, shrink_weight))[0].astype(jnp.bfloat16)
    g_expand_weight = rows_product(normed_m, grad_hidden)
    g_expand_bias = jnp.sum(grad_hidden.astype(jnp.float32), 0)
    space_grad, g_mlp_gain, g_mlp_shift = norm_m_back(back_product(grad_hidden, expand_weight))
    space_grad = cotan + space_grad
    grad_ys = space_grad.astype(jnp.bfloat16)
    g_spatial_out = rows_product(mixed_s, grad_ys)
    g_spatial_bias = jnp.sum(grad_ys.astype(jnp.float32), 0)
    grad_mixed_s = back_product(grad_ys, spatial_out).astype(jnp.bfloat16).reshape(head_shape)
    again_s = jnp.exp(
        jnp.einsum("cfphd,cfrhd->cfhpr", query_s, key_s, preferred_element_type=jnp.float32) * 0.125
        - lse_s
    )
    grad_probs_s = jnp.einsum(
        "cfphd,cfrhd->cfhpr", grad_mixed_s, value_s, preferred_element_type=jnp.float32
    )
    grad_scores_s = softmax_back(again_s, grad_probs_s)
    grad_query_s = (
        jnp.einsum("cfhpr,cfrhd->cfphd", grad_scores_s, key_s, preferred_element_type=jnp.float32)
        * 0.125
    ).astype(jnp.bfloat16)
    grad_key_s = (
        jnp.einsum("cfhpr,cfphd->cfrhd", grad_scores_s, query_s, preferred_element_type=jnp.float32)
        * 0.125
    ).astype(jnp.bfloat16)
    grad_value_s = jnp.einsum(
        "cfhpr,cfphd->cfrhd",
        again_s.astype(jnp.bfloat16),
        grad_mixed_s,
        preferred_element_type=jnp.float32,
    ).astype(jnp.bfloat16)
    grad_packed_s = jnp.stack([grad_query_s, grad_key_s, grad_value_s], axis=3).reshape(
        row_count, 3 * model_width
    )
    g_spatial_in = rows_product(normed_s, grad_packed_s)
    time_grad, g_spatial_gain, g_spatial_shift = norm_s_back(
        back_product(grad_packed_s, spatial_in)
    )
    time_grad = space_grad + time_grad
    grad_yt = time_grad.astype(jnp.bfloat16)
    g_temporal_out = rows_product(mixed_t, grad_yt)
    g_temporal_bias = jnp.sum(grad_yt.astype(jnp.float32), 0)
    grad_mixed_flat = back_product(grad_yt, temporal_out).astype(jnp.bfloat16)
    grad_rows = lax.all_to_all(
        to_patch_rows(grad_mixed_flat, slot_count, local_frames, patch_count),
        "frame",
        split_axis=0,
        concat_axis=1,
        tiled=True,
    )
    grad_mixed_x = grad_rows.reshape(split_shape)
    again_x = jnp.exp(
        jnp.einsum("rfhd,rghd->rhfg", query_x, key_x, preferred_element_type=jnp.float32) * 0.125
        - lse_x
    )
    grad_probs_x = jnp.einsum(
        "rfhd,rghd->rhfg", grad_mixed_x, value_x, preferred_element_type=jnp.float32
    )
    grad_scores_x = softmax_back(again_x, grad_probs_x)
    grad_query_x = (
        jnp.einsum("rhfg,rghd->rfhd", grad_scores_x, key_x, preferred_element_type=jnp.float32)
        * 0.125
    ).astype(jnp.bfloat16)
    grad_key_x = (
        jnp.einsum("rhfg,rfhd->rghd", grad_scores_x, query_x, preferred_element_type=jnp.float32)
        * 0.125
    ).astype(jnp.bfloat16)
    grad_value_x = jnp.einsum(
        "rhfg,rfhd->rghd",
        again_x.astype(jnp.bfloat16),
        grad_mixed_x,
        preferred_element_type=jnp.float32,
    ).astype(jnp.bfloat16)
    packed_width = (row_part, all_frames, model_width)
    grad_stacked = jnp.concatenate(
        [
            grad_query_x.reshape(packed_width),
            grad_key_x.reshape(packed_width),
            grad_value_x.reshape(packed_width),
        ],
        axis=2,
    )
    grad_back = lax.all_to_all(grad_stacked, "frame", split_axis=1, concat_axis=0, tiled=True)
    grad_packed_t = from_patch_rows(grad_back, slot_count, local_frames, patch_count)
    g_temporal_in = rows_product(normed_t, grad_packed_t)
    input_grad, g_temporal_gain, g_temporal_shift = norm_t_back(
        back_product(grad_packed_t, temporal_in)
    )
    input_grad = time_grad + input_grad
    grads = (
        g_temporal_gain,
        g_temporal_shift,
        g_temporal_in,
        g_temporal_out,
        g_temporal_bias,
        g_spatial_gain,
        g_spatial_shift,
        g_spatial_in,
        g_spatial_out,
        g_spatial_bias,
        g_mlp_gain,
        g_mlp_shift,
        g_expand_weight,
        g_expand_bias,
        g_shrink_weight,
        g_shrink_bias,
    )
    return (
        block_rows.astype(jnp.bfloat16).reshape(tokens.shape),
        input_grad.astype(jnp.bfloat16).reshape(tokens.shape),
        grads,
    )


def generic_body(
    patch_tokens,
    live_slots,
    out_grad,
    temporal_gain,
    temporal_shift,
    temporal_in,
    temporal_out,
    temporal_bias,
    spatial_gain,
    spatial_shift,
    spatial_in,
    spatial_out,
    spatial_bias,
    mlp_gain,
    mlp_shift,
    expand_weight,
    expand_bias,
    shrink_weight,
    shrink_bias,
):
    shards = (
        temporal_gain,
        temporal_shift,
        temporal_in,
        temporal_out,
        temporal_bias,
        spatial_gain,
        spatial_shift,
        spatial_in,
        spatial_out,
        spatial_bias,
        mlp_gain,
        mlp_shift,
        expand_weight,
        expand_bias,
        shrink_weight,
        shrink_bias,
    )
    devices = lax.axis_size("clip") * lax.axis_size("frame")
    start = tuple(
        (
            jnp.zeros((member.shape[0] * devices,) + member.shape[1:], jnp.float32)
            for member in shards
        )
    )

    def one_step(totals, inputs):
        tokens, out_cot, count = inputs
        weights = (
            lax.all_gather(temporal_gain, ("clip", "frame"), axis=0, tiled=True),
            lax.all_gather(temporal_shift, ("clip", "frame"), axis=0, tiled=True),
            lax.all_gather(temporal_in, ("clip", "frame"), axis=0, tiled=True),
            lax.all_gather(temporal_out, ("clip", "frame"), axis=0, tiled=True),
            lax.all_gather(temporal_bias, ("clip", "frame"), axis=0, tiled=True),
            lax.all_gather(spatial_gain, ("clip", "frame"), axis=0, tiled=True),
            lax.all_gather(spatial_shift, ("clip", "frame"), axis=0, tiled=True),
            lax.all_gather(spatial_in, ("clip", "frame"), axis=0, tiled=True),
            lax.all_gather(spatial_out, ("clip", "frame"), axis=0, tiled=True),
            lax.all_gather(spatial_bias, ("clip", "frame"), axis=0, tiled=True),
            lax.all_gather(mlp_gain, ("clip", "frame"), axis=0, tiled=True),
            lax.all_gather(mlp_shift, ("clip", "frame"), axis=0, tiled=True),
            lax.all_gather(expand_weight, ("clip", "frame"), axis=0, tiled=True),
            lax.all_gather(expand_bias, ("clip", "frame"), axis=0, tiled=True),
            lax.all_gather(shrink_weight, ("clip", "frame"), axis=0, tiled=True),
            lax.all_gather(shrink_bias, ("clip", "frame"), axis=0, tiled=True),
        )
        block_part, grad_part, grads = micro_batch(weights, tokens, out_cot, count)
        totals = tuple((summed + addend for summed, addend in zip(totals, grads)))
        return (totals, (block_part, grad_part))

    totals, outputs = lax.scan(one_step, start, (patch_tokens, out_grad, live_slots[:, 0]))
    block_out, patch_grad = outputs
    totals = (
        lax.psum_scatter(totals[0], ("clip", "frame"), scatter_dimension=0, tiled=True),
        lax.psum_scatter(totals[1], ("clip", "frame"), scatter_dimension=0, tiled=True),
        lax.psum_scatter(totals[2], ("clip", "frame"), scatter_dimension=0, tiled=True),
        lax.psum_scatter(totals[3], ("clip", "frame"), scatter_dimension=0, tiled=True),
        lax.psum_scatter(totals[4], ("clip", "frame"), scatter_dimension=0, tiled=True),
        lax.psum_scatter(totals[5], ("clip", "frame"), scatter_dimension=0, tiled=True),
        lax.psum_scatter(totals[6], ("clip", "frame"), scatter_dimension=0, tiled=True),
        lax.psum_scatter(totals[7], ("clip", "frame"), scatter_dimension=0, tiled=True),
        lax.psum_scatter(totals[8], ("clip", "frame"), scatter_dimension=0, tiled=True),
        lax.psum_scatter(totals[9], ("clip", "frame"), scatter_dimension=0, tiled=True),
        lax.psum_scatter(totals[10], ("clip", "frame"), scatter_dimension=0, tiled=True),
        lax.psum_scatter(totals[11], ("clip", "frame"), scatter_dimension=0, tiled=True),
        lax.psum_scatter(totals[12], ("clip", "frame"), scatter_dimension=0, tiled=True),
        lax.psum_scatter(totals[13], ("clip", "frame"), scatter_dimension=0, tiled=True),
        lax.psum_scatter(totals[14], ("clip", "frame"), scatter_dimension=0, tiled=True),
        lax.psum_scatter(totals[15], ("clip", "frame"), scatter_dimension=0, tiled=True),
    )
    return (block_out, patch_grad) + tuple(totals)


def nn(left, right):
    return lax.dot_general(left, right, (((1,), (0,)), ((), ())), preferred_element_type=f32)


def nt(left, right):
    return lax.dot_general(left, right, (((1,), (1,)), ((), ())), preferred_element_type=f32)


def tn(left, right):
    return lax.dot_general(left, right, (((0,), (0,)), ((), ())), preferred_element_type=f32)


TAIL_POLE = 0.275
TAIL = (0.11782574, 0.04201021, 0.33417963, -0.33129375, 0.45218007, -0.1149019)


def gelu_parts(u):
    bell = jnp.exp(u * u * -0.5)
    t = 1.0 / (1.0 + TAIL_POLE * jnp.abs(u))
    poly = jnp.full_like(t, TAIL[5])
    for term in TAIL[4::-1]:
        poly = poly * t + term
    tail = poly * t * bell
    cdf = jnp.where(u >= 0, 1.0 - tail, tail)
    return u * cdf, cdf + u * (bell * 0.3989422804014327)


def norm_parts(v):
    centre = v - jnp.mean(v, -1, keepdims=True)
    r = lax.rsqrt(jnp.mean(centre * centre, -1, keepdims=True) + 1e-06)
    return centre * r, r


def norm_back(a, n, r, gain):
    scaled = a * gain
    return r * (
        scaled
        - jnp.mean(scaled, -1, keepdims=True)
        - n * jnp.mean(scaled * n, -1, keepdims=True)
    )


def column_sum(values):
    return jnp.sum(values, 0, keepdims=True)


def halves(pair):
    lane = lax.broadcasted_iota(jnp.int32, pair.shape, 1)
    zero = jnp.zeros_like(pair)
    return jnp.where(lane < DH, pair, zero), jnp.where(lane < DH, zero, pair)


def stacked(pair):
    return jnp.concatenate(halves(pair), axis=0)


T_GAIN, T_SHIFT, T_BIAS, S_GAIN, S_SHIFT, S_BIAS, M_GAIN, M_SHIFT, M_BIAS, HIDDEN = range(10)


def row_of(ref, at):
    return ref[at : at + 1, :]


def lanes(start, size):
    return pl.ds(pl.multiple_of(start, size), size)


def temporal_forward_kernel(
    slot_ref, own_ref, other_ref, vec_ref, win_ref,
    packed_ref, probs_ref, mixed_own_ref, mixed_other_ref, pad_s,
):
    pad_s[...] = jnp.zeros_like(pad_s)
    gain, shift = row_of(vec_ref, T_GAIN), row_of(vec_ref, T_SHIFT)
    for half, tokens_ref in enumerate((own_ref, other_ref)):

        def project(i, carry, half=half, tokens_ref=tokens_ref):
            for f in range(PAIR):
                pad_s[f, :PATCHES] = tokens_ref[PAIR * i + f]
            n, _ = norm_parts(pad_s[...].reshape(TILE, D).astype(f32))
            normed = (n * gain + shift).astype(bf16)
            at = pl.ds(half * 4 + PAIR * i, PAIR)
            packed_ref[at] = nn(normed, win_ref[...]).astype(bf16).reshape(PAIR, ROWS, 3 * D)
            return carry

        lax.fori_loop(0, 4 // PAIR, project, 0)

    row = lax.broadcasted_iota(jnp.int32, (8 * BLOCK, 8 * BLOCK), 0) % BLOCK
    col = lax.broadcasted_iota(jnp.int32, (8 * BLOCK, 8 * BLOCK), 1) % BLOCK
    same = row == col

    def attend(b, carry):
        at = pl.ds(pl.multiple_of(b * BLOCK, BLOCK), BLOCK)
        def part(h, k):
            lo = k * D + 128 * h
            return packed_ref[:, at, lo : lo + 128].reshape(8 * BLOCK, 128)

        scores, both = [], []
        for h in range(H // 2):
            query = part(h, 0) * jnp.asarray(0.125, bf16)
            scores.append(nt(query, stacked(part(h, 1))))
        for h in range(H // 2):
            probs = []
            for k in range(2):
                s = jnp.where(same, scores[h][:, 128 * k : 128 * k + 128], -1e30)
                e = jnp.exp(s - jnp.max(s, -1, keepdims=True))
                probs.append(e * (1.0 / jnp.sum(e, -1, keepdims=True)))
            both.append(jnp.concatenate(probs, axis=1).astype(bf16))
            probs_ref[b, h] = both[h]
        for h in range(H // 2):
            mixed = nn(both[h], stacked(part(h, 2))).astype(bf16).reshape(8, BLOCK, 128)
            mixed_own_ref[:, at, 128 * h : 128 * h + 128] = mixed[:4]
            mixed_other_ref[:, at, 128 * h : 128 * h + 128] = mixed[4:]
        return carry

    lax.fori_loop(0, BLOCKS, attend, 0)


def fixed(shape, at=None):
    at = at or (0,) * len(shape)
    return pl.BlockSpec(shape, lambda *ids: at, pipeline_mode=pl.Buffered(1))


def out_of(shape, kind):
    return jax.ShapeDtypeStruct(shape, kind)


def temporal_forward(slot, tokens, other, vec, weights):
    mbs = tokens.shape[0]
    frames = tokens.shape[2]
    own = pl.BlockSpec((None, None, frames, PATCHES, D), lambda m, s: (m, s[0], 0, 0, 0))
    mixed = pl.BlockSpec((None, frames, ROWS, D), lambda m, s: (m, 0, 0, 0))
    return pl.pallas_call(
        temporal_forward_kernel,
        grid_spec=pltpu.PrefetchScalarGridSpec(
            num_scalar_prefetch=1,
            grid=(mbs,),
            in_specs=[
                own,
                pl.BlockSpec((None, frames, PATCHES, D), lambda m, s: (m, 0, 0, 0)),
                fixed((16, D)),
                fixed((D, 3 * D)),
            ],
            out_specs=[
                pl.BlockSpec((None, 8, ROWS, 3 * D), lambda m, s: (m, 0, 0, 0)),
                pl.BlockSpec((None, BLOCKS, H // 2, 128, 256), lambda m, s: (m, 0, 0, 0, 0)),
                mixed,
                mixed,
            ],
            scratch_shapes=[pltpu.VMEM((PAIR, ROWS, D), bf16)],
        ),
        out_shape=[
            out_of((mbs, 8, ROWS, 3 * D), bf16),
            out_of((mbs, BLOCKS, H // 2, 128, 256), bf16),
            out_of((mbs, frames, ROWS, D), bf16),
            out_of((mbs, frames, ROWS, D), bf16),
        ],
        compiler_params=pltpu.CompilerParams(vmem_limit_bytes=VMEM_BYTES),
        cost_estimate=pl.CostEstimate(
            flops=2 * mbs * 8 * ROWS * D * 4 * D, bytes_accessed=60 << 20, transcendentals=0
        ),
        name="temporal_forward",
    )(slot, tokens, other, vec, weights)


def spatial_forward_kernel(*refs):
    slot_ref, tokens_ref, mixed_ref, vec_ref, tout_ref, sin_ref, sout_ref = refs[:7]
    time_ref, packed_ref, probs_ref, mixs_ref, space_ref, pad_s = refs[-6:]
    pad_s[...] = jnp.zeros_like(pad_s)
    for f in range(PAIR):
        pad_s[f, :PATCHES] = tokens_ref[f]
    tokens = pad_s[...].reshape(TILE, D).astype(f32)
    time = tokens + nn(mixed_ref[...].reshape(TILE, D), tout_ref[...]) + row_of(vec_ref, T_BIAS)
    time_ref[...] = time.reshape(PAIR, ROWS, D)
    n, _ = norm_parts(time)
    normed = (n * row_of(vec_ref, S_GAIN) + row_of(vec_ref, S_SHIFT)).astype(bf16)
    packed_ref[...] = nn(normed, sin_ref[...]).astype(bf16).reshape(PAIR, ROWS, 3 * D)
    valid = lax.broadcasted_iota(jnp.int32, (ROWS, ROWS), 1) < PATCHES

    def attend(g, carry):
        both = [(f, GROUP * g + i) for i in range(GROUP) for f in range(PAIR)]

        def part(f, h, k):
            return packed_ref[f, :, lanes(k * D + 128 * h, 128)]

        scores, probs = [], []
        for f, h in both:
            query = part(f, h, 0) * jnp.asarray(0.125, bf16)
            scores += [nt(query, keys) for keys in halves(part(f, h, 1))]
        for i, s in enumerate(scores):
            f, h = both[i // 2]
            s = jnp.where(valid, s, -1e30)
            e = jnp.exp(s - jnp.max(s, -1, keepdims=True))
            probs.append((e * (1.0 / jnp.sum(e, -1, keepdims=True))).astype(bf16))
            probs_ref[f, 2 * h + i % 2] = probs[i]
        for i, (f, h) in enumerate(both):
            low, high = halves(part(f, h, 2))
            total = nn(probs[2 * i], low) + nn(probs[2 * i + 1], high)
            mixs_ref[f, :, lanes(128 * h, 128)] = total.astype(bf16)
        return carry

    lax.fori_loop(0, H // 2 // GROUP, attend, 0)
    mixed = mixs_ref[...].reshape(TILE, D)
    space_ref[...] = (
        time_ref[...].reshape(TILE, D) + nn(mixed, sout_ref[...]) + row_of(vec_ref, S_BIAS)
    ).reshape(PAIR, ROWS, D)


def spatial_forward(which, slot, tokens, mixed, vec, second, earlier):
    mbs, slots, frames = tokens.shape[:3]

    def framed(*tail):
        return pl.BlockSpec(
            (None, None, PAIR) + tail, lambda m, i, s: (which, m, i) + (0,) * len(tail)
        )

    def whole(*tail):
        return (slots, mbs, frames) + tail

    shapes = [
        out_of(whole(ROWS, D), f32),
        out_of(whole(ROWS, 3 * D), bf16),
        out_of(whole(H, ROWS, ROWS), bf16),
        out_of(whole(ROWS, D), bf16),
        out_of(whole(ROWS, D), f32),
    ]
    return pl.pallas_call(
        spatial_forward_kernel,
        grid_spec=pltpu.PrefetchScalarGridSpec(
            num_scalar_prefetch=1,
            grid=(mbs, frames // PAIR),
            in_specs=[
                pl.BlockSpec(
                    (None, None, PAIR, PATCHES, D), lambda m, i, s: (m, s[which], i, 0, 0)
                ),
                pl.BlockSpec((None, PAIR, ROWS, D), lambda m, i, s: (m, i, 0, 0)),
                fixed((16, D)),
                fixed((D, D), (0, 3)),
                fixed((D, 3 * D)),
                fixed((D, D), (0, 4)),
            ]
            + [pl.BlockSpec(memory_space=pl.ANY)] * len(earlier),
            out_specs=[
                framed(ROWS, D),
                framed(ROWS, 3 * D),
                framed(H, ROWS, ROWS),
                framed(ROWS, D),
                framed(ROWS, D),
            ],
            scratch_shapes=[pltpu.VMEM((PAIR, ROWS, D), bf16)],
        ),
        out_shape=shapes,
        input_output_aliases={7 + i: i for i in range(len(earlier))},
        compiler_params=pltpu.CompilerParams(vmem_limit_bytes=VMEM_BYTES),
        cost_estimate=pl.CostEstimate(
            flops=2 * mbs * frames * ROWS * D * 6 * D, bytes_accessed=60 << 20, transcendentals=0
        ),
        name="spatial_forward",
    )(slot, tokens, mixed, vec, second, second, second, *earlier)


def mlp_kernel(
    slot_ref, live_ref, space_ref, cotan_ref, vec_ref, hidden_ref, expand_ref, shrink_ref,
    out_ref, grad_ref, weights_ref, sums_ref, hidden_sums_ref,
    z_s, normed_s, total_s, back_s, expand_s, shrink_s,
):
    i = pl.program_id(0)

    @pl.when(i == 0)
    def _():
        expand_s[...] = jnp.zeros_like(expand_s)
        shrink_s[...] = jnp.zeros_like(shrink_s)
        sums_ref[...] = jnp.zeros_like(sums_ref)
        hidden_sums_ref[...] = jnp.zeros_like(hidden_sums_ref)
        z_s[...] = jnp.zeros_like(z_s)

    gain = row_of(vec_ref, M_GAIN)
    live = live_ref[i]
    for f in range(PAIR):
        cotan = cotan_ref[f]
        z_s[f, :PATCHES] = jnp.where(live > 0, cotan, jnp.zeros_like(cotan))
    grad_z = z_s[...].reshape(TILE, D)
    space = space_ref[...].reshape(TILE, D)
    n, _ = norm_parts(space)
    normed = (n * gain + row_of(vec_ref, M_SHIFT)).astype(bf16)
    normed_s[...] = normed
    total_s[...] = space + row_of(vec_ref, M_BIAS)
    back_s[...] = jnp.zeros_like(back_s)
    normed_turned = normed.T
    z_turned = grad_z.T

    def ahead(j):
        at = slice(j * CHUNK, (j + 1) * CHUNK)
        hidden = nn(normed_s[...], expand_ref[:, at]) + hidden_ref[:, at]
        return hidden, nt(grad_z, shrink_ref[:, at])

    pending = ahead(0)
    for j in range(CHUNKS):
        at = slice(j * CHUNK, (j + 1) * CHUNK)
        hidden, grad_active = pending
        if j + 1 < CHUNKS:
            pending = ahead(j + 1)
        active, slope = gelu_parts(hidden)
        active = active.astype(bf16)
        grad_hidden = (slope * grad_active).astype(bf16)
        total_s[...] += nn(active, shrink_ref[:, at])
        shrink_s[:, at] += nn(z_turned, active)
        expand_s[:, at] += nn(normed_turned, grad_hidden)
        back_s[...] += nt(grad_hidden, expand_ref[:, at])
        hidden_sums_ref[0:1, at] += column_sum(grad_hidden.astype(f32))
    block_out = total_s[...].reshape(PAIR, ROWS, D)
    for f in range(PAIR):
        out_ref[f] = block_out[f, :PATCHES].astype(bf16)
    a = back_s[...]
    n, r = norm_parts(space_ref[...].reshape(TILE, D))
    wide_z = grad_z.astype(f32)
    grad_ref[...] = (wide_z + norm_back(a, n, r, gain)).reshape(PAIR, ROWS, D)
    sums_ref[0:1] += column_sum(a * n)
    sums_ref[1:2] += column_sum(a)
    sums_ref[2:3] += column_sum(wide_z)

    @pl.when(i == pl.num_programs(0) - 1)
    def _():
        weights_ref[:, : CHUNKS * CHUNK] = expand_s[...].astype(bf16)
        for j in range(CHUNKS):
            lo = j * CHUNK
            weights_ref[:, CHUNKS * CHUNK + lo : CHUNKS * CHUNK + lo + D] = (
                shrink_s[:, lo : lo + CHUNK].T.astype(bf16)
            )


def mlp(slot, live, space, cotan, vec, hidden, third):
    slots, mbs, frames = space.shape[:3]
    per = frames // PAIR
    steps = slots * mbs * per

    def placed(i):
        return i // (mbs * per), (i // per) % mbs, i % per

    def by_slot(i, s, live):
        r, m, f = placed(i)
        return m, s[r], f, 0, 0

    def framed(i, s, live):
        return placed(i) + (0, 0)

    outer = pl.BlockSpec((None, None, PAIR, PATCHES, D), by_slot)
    inner = pl.BlockSpec((None, None, PAIR, ROWS, D), framed)
    width = CHUNKS * CHUNK
    return pl.pallas_call(
        mlp_kernel,
        grid_spec=pltpu.PrefetchScalarGridSpec(
            num_scalar_prefetch=2,
            grid=(steps,),
            in_specs=[
                inner,
                outer,
                fixed((16, D)),
                fixed((1, width)),
                fixed((D, width), (0, 0)),
                fixed((D, width), (0, 1)),
            ],
            out_specs=[
                outer,
                inner,
                fixed((D, 2 * width)),
                fixed((8, D)),
                fixed((8, width)),
            ],
            scratch_shapes=[
                pltpu.VMEM((PAIR, ROWS, D), bf16),
                pltpu.VMEM((TILE, D), bf16),
                pltpu.VMEM((TILE, D), f32),
                pltpu.VMEM((TILE, D), f32),
                pltpu.VMEM((D, width), f32),
                pltpu.VMEM((D, width), f32),
            ],
        ),
        out_shape=[
            out_of(cotan.shape, bf16),
            out_of(space.shape, f32),
            out_of((D, 2 * width), bf16),
            out_of((8, D), f32),
            out_of((8, width), f32),
        ],
        compiler_params=pltpu.CompilerParams(vmem_limit_bytes=VMEM_BYTES),
        cost_estimate=pl.CostEstimate(
            flops=12 * steps * TILE * D * width, bytes_accessed=60 << 20, transcendentals=0
        ),
        name="mlp",
    )(slot, live, space, cotan, vec, hidden, third, third)


def spatial_backward_kernel(first_call, *refs):
    (
        grad_ref, packed_ref, probs_ref, mixs_ref, time_ref, mixed_ref,
        vec_ref, tout_ref, sin_ref, sout_ref,
    ) = refs[:10]
    if first_call:
        weights_ref, sums_ref, time_grad_ref, back_ref, gmix_s, gpack_s = refs[-6:]
        total = weights_ref
    else:
        total_ref, sums_before_ref = refs[10:12]
        weights_ref, sums_ref, time_grad_ref, back_ref, gmix_s, gpack_s, total, copied = refs[-8:]
        taken = pltpu.make_async_copy(total_ref, total, copied)
    step = pl.program_id(0) * pl.num_programs(1) + pl.program_id(1)
    steps = pl.num_programs(0) * pl.num_programs(1)

    @pl.when(step == 0)
    def _():
        if first_call:
            total[...] = jnp.zeros_like(total)
            sums_ref[...] = jnp.zeros_like(sums_ref)
        else:
            taken.start()
            sums_ref[...] = sums_before_ref[...]

    gain = row_of(vec_ref, S_GAIN)
    space_grad = grad_ref[...].reshape(TILE, D)
    grad_ys = space_grad.astype(bf16)
    gmix_s[...] = nt(grad_ys, sout_ref[...]).astype(bf16).reshape(PAIR, ROWS, D)

    def attend(g, carry):
        both = [(f, BACK_GROUP * g + i) for i in range(BACK_GROUP) for f in range(PAIR)]

        def part(f, h, k):
            return packed_ref[f, :, lanes(k * D + 128 * h, 128)]

        products, scores = [], []
        for f, h in both:
            out_pair = gmix_s[f, :, lanes(128 * h, 128)]
            products += [nt(out_pair, values) for values in halves(part(f, h, 2))]
        for i, product in enumerate(products):
            f, h = both[i // 2]
            wide = probs_ref[f, 2 * h + i % 2].astype(f32)
            product = wide * product
            scores.append(
                (product - wide * jnp.sum(product, -1, keepdims=True)).astype(bf16)
            )
        for i, (f, h) in enumerate(both):
            outs = halves(gmix_s[f, :, lanes(128 * h, 128)])
            queries, keys = halves(part(f, h, 0)), halves(part(f, h, 1))
            near = scores[2 * i : 2 * i + 2]
            grad_v = tn(probs_ref[f, 2 * h], outs[0]) + tn(probs_ref[f, 2 * h + 1], outs[1])
            grad_q = nn(near[0], keys[0]) + nn(near[1], keys[1])
            grad_k = tn(near[0], queries[0]) + tn(near[1], queries[1])
            gpack_s[f, :, lanes(128 * h, 128)] = (grad_q * 0.125).astype(bf16)
            gpack_s[f, :, lanes(D + 128 * h, 128)] = (grad_k * 0.125).astype(bf16)
            gpack_s[f, :, lanes(2 * D + 128 * h, 128)] = grad_v.astype(bf16)
        return carry

    lax.fori_loop(0, H // 2 // BACK_GROUP, attend, 0)
    if not first_call:
        pl.when(step == 0)(taken.wait)
    total[:, 3 * D : 4 * D] += tn(mixs_ref[...].reshape(TILE, D), grad_ys)
    n, r = norm_parts(time_ref[...].reshape(TILE, D))
    normed = (n * gain + row_of(vec_ref, S_SHIFT)).astype(bf16)
    grad_packed = gpack_s[...].reshape(TILE, 3 * D)
    total[:, : 3 * D] += tn(normed, grad_packed)
    a = nt(grad_packed, sin_ref[...])
    time_grad = grad_ref[...].reshape(TILE, D) + norm_back(a, n, r, gain)
    time_grad_ref[...] = time_grad.reshape(PAIR, ROWS, D)
    grad_yt = time_grad.astype(bf16)
    total[:, 4 * D :] += tn(mixed_ref[...].reshape(TILE, D), grad_yt)
    back_ref[...] = nt(grad_yt, tout_ref[...]).astype(bf16).reshape(PAIR, ROWS, D)
    sums_ref[0:1] += column_sum(a * n)
    sums_ref[1:2] += column_sum(a)
    sums_ref[2:3] += column_sum(grad_ys.astype(f32))
    sums_ref[3:4] += column_sum(grad_yt.astype(f32))
    if not first_call:

        @pl.when(step == steps - 1)
        def _():
            weights_ref[...] = total[...].astype(bf16)


def spatial_backward(which, grad, packed, probs, mixs, time, mixed, vec, second, earlier):
    slots, mbs, frames = grad.shape[:3]

    def framed(*tail):
        return pl.BlockSpec(
            (None, None, PAIR) + tail, lambda m, i: (which, m, i) + (0,) * len(tail)
        )

    single = pl.BlockSpec((None, PAIR, ROWS, D), lambda m, i: (m, i, 0, 0))
    scratch = [pltpu.VMEM((PAIR, ROWS, D), bf16), pltpu.VMEM((PAIR, ROWS, 3 * D), bf16)]
    extra = []
    if earlier:
        extra = [pl.BlockSpec(memory_space=pl.ANY), fixed((8, D))]
        scratch = scratch + [pltpu.VMEM((D, 5 * D), f32), pltpu.SemaphoreType.DMA(())]

    def kernel(*refs):
        return spatial_backward_kernel(not earlier, *refs)

    return pl.pallas_call(
        kernel,
        grid=(mbs, frames // PAIR),
        in_specs=[
            framed(ROWS, D),
            framed(ROWS, 3 * D),
            framed(H, ROWS, ROWS),
            framed(ROWS, D),
            framed(ROWS, D),
            single,
            fixed((16, D)),
            fixed((D, D), (0, 3)),
            fixed((D, 3 * D)),
            fixed((D, D), (0, 4)),
        ]
        + extra,
        out_specs=[fixed((D, 5 * D)), fixed((8, D)), single, single],
        out_shape=[
            out_of((D, 5 * D), bf16 if earlier else f32),
            out_of((8, D), f32),
            out_of((mbs, frames, ROWS, D), f32),
            out_of((mbs, frames, ROWS, D), bf16),
        ],
        scratch_shapes=scratch,
        compiler_params=pltpu.CompilerParams(vmem_limit_bytes=VMEM_BYTES),
        cost_estimate=pl.CostEstimate(
            flops=2 * mbs * frames * ROWS * D * 14 * D, bytes_accessed=60 << 20, transcendentals=0
        ),
        name="spatial_backward",
    )(grad, packed, probs, mixs, time, mixed, vec, second, second, second, *earlier)


def temporal_backward_kernel(
    slot_ref, own_ref, other_ref, packed_ref, probs_ref, back_own_ref, back_other_ref,
    vec_ref, win_ref, space_sums_ref, mlp_sums_ref, hidden_sums_ref, space_ref,
    weights_ref, gpack_ref, pad_s, total_s, sums_s, columns_s, copied,
):
    m, j = pl.program_id(0), pl.program_id(1)
    taken = pltpu.make_async_copy(space_ref, weights_ref.at[:, 3 * D + 128 :], copied)

    @pl.when((m == 0) & (j == 0))
    def _():
        taken.start()
        total_s[...] = jnp.zeros_like(total_s)
        columns_s[...] = jnp.zeros_like(columns_s)
        sums_s[...] = jnp.zeros_like(sums_s)
        sums_s[T_BIAS : T_BIAS + 1] = space_sums_ref[3:4]
        sums_s[S_GAIN : S_GAIN + 3] = space_sums_ref[0:3]
        sums_s[M_GAIN : M_GAIN + 3] = mlp_sums_ref[0:3]
        for k in range(CHUNKS):
            sums_s[HIDDEN + k : HIDDEN + k + 1] = hidden_sums_ref[0:1, k * D : (k + 1) * D]
        sums_s[16:32] = vec_ref[...]
        pad_s[...] = jnp.zeros_like(pad_s)

    @pl.when(j < BLOCKS)
    def _():
        at = pl.ds(pl.multiple_of(jnp.minimum(j, BLOCKS - 1) * BLOCK, BLOCK), BLOCK)

        def part(h, k):
            lo = k * D + 128 * h
            return packed_ref[:, :, lo : lo + 128].reshape(8 * BLOCK, 128)

        def out_pair(h):
            lo = 128 * h
            return jnp.concatenate(
                [back_own_ref[:, :, lo : lo + 128], back_other_ref[:, :, lo : lo + 128]], axis=0
            ).reshape(8 * BLOCK, 128)

        products = [nt(out_pair(h), stacked(part(h, 2))) for h in range(H // 2)]
        scores = []
        for h in range(H // 2):
            wide = probs_ref[h].astype(f32)
            product = wide * products[h]
            pair = []
            for k in range(2):
                near = product[:, 128 * k : 128 * k + 128]
                weight = wide[:, 128 * k : 128 * k + 128]
                pair.append((near - weight * jnp.sum(near, -1, keepdims=True)).astype(bf16))
            scores.append(pair)
        for h in range(H // 2):
            lo = 128 * h
            probs = probs_ref[h]
            grad_v = tn(
                jnp.concatenate([probs[:, :128], probs[:, 128:]], axis=0), stacked(out_pair(h))
            )
            grad_q = nn(jnp.concatenate(scores[h], axis=1), stacked(part(h, 1))) * 0.125
            grad_k = tn(jnp.concatenate(scores[h], axis=0), stacked(part(h, 0))) * 0.125
            for k, values_of in enumerate((grad_q, grad_k, grad_v)):
                gpack_ref[:, at, k * D + lo : k * D + lo + 128] = values_of.astype(bf16).reshape(
                    8, BLOCK, 128
                )

    @pl.when(j >= BLOCKS)
    def _():
        p = jnp.clip(j - BLOCKS, 0, 1)
        for f in range(HALF):
            pad_s[f, :PATCHES] = jnp.where(p == 0, own_ref[f], other_ref[f])
        n, _ = norm_parts(pad_s[...].reshape(HALF * ROWS, D).astype(f32))
        grad_packed = gpack_ref[pl.ds(HALF * p, HALF)].reshape(HALF * ROWS, 3 * D)
        total_s[...] += tn(n.astype(bf16), grad_packed)
        columns_s[0:1] += column_sum(grad_packed.astype(f32))

    @pl.when((m == pl.num_programs(0) - 1) & (j == pl.num_programs(1) - 1))
    def _():
        taken.wait()
        turned = sums_s[...].T
        gain, shift = turned[:, 16 + T_GAIN : 17 + T_GAIN], turned[:, 16 + T_SHIFT : 17 + T_SHIFT]
        g_gain = jnp.zeros((D, 1), f32)
        g_shift = jnp.zeros((D, 1), f32)
        for k in range(3):
            at = slice(k * D, (k + 1) * D)
            total, columns = total_s[:, at], columns_s[0:1, at]
            win = win_ref[:, at].astype(f32)
            weights_ref[:, at] = (gain * total + shift * columns).astype(bf16)
            g_gain = g_gain + jnp.sum(total * win, -1, keepdims=True)
            g_shift = g_shift + jnp.sum(columns * win, -1, keepdims=True)
        lane = lax.broadcasted_iota(jnp.int32, (D, 128), 1)
        turned = jnp.where(lane == T_GAIN, g_gain, jnp.where(lane == T_SHIFT, g_shift, turned))
        weights_ref[:, 3 * D : 3 * D + 128] = turned.astype(bf16)


def temporal_backward(
    slot, tokens, other, packed, probs, back_own, back_other, vec, weights,
    space_sums, mlp_sums, hidden_sums, space,
):
    mbs, slots, frames = tokens.shape[:3]
    def row_block(j):
        return jnp.minimum(j, BLOCKS - 1)

    rows_of = pl.BlockSpec((None, frames, BLOCK, D), lambda m, j, s: (m, 0, row_block(j), 0))
    return pl.pallas_call(
        temporal_backward_kernel,
        grid_spec=pltpu.PrefetchScalarGridSpec(
            num_scalar_prefetch=1,
            grid=(mbs, BLOCKS + 2),
            in_specs=[
                pl.BlockSpec((None, None, HALF, PATCHES, D), lambda m, j, s: (m, s[0], 0, 0, 0)),
                pl.BlockSpec((None, HALF, PATCHES, D), lambda m, j, s: (m, 0, 0, 0)),
                pl.BlockSpec((None, 8, BLOCK, 3 * D), lambda m, j, s: (m, 0, row_block(j), 0)),
                pl.BlockSpec(
                    (None, None, H // 2, 128, 256), lambda m, j, s: (m, row_block(j), 0, 0, 0)
                ),
                rows_of,
                rows_of,
                fixed((16, D)),
                fixed((D, 3 * D)),
                fixed((8, D)),
                fixed((8, D)),
                fixed((8, CHUNKS * D)),
                pl.BlockSpec(memory_space=pl.ANY),
            ],
            out_specs=[
                fixed((D, 8 * D + 128)),
                pl.BlockSpec((None, 8, ROWS, 3 * D), lambda m, j, s: (m, 0, 0, 0)),
            ],
            scratch_shapes=[
                pltpu.VMEM((HALF, ROWS, D), bf16),
                pltpu.VMEM((D, 3 * D), f32),
                pltpu.VMEM((128, D), f32),
                pltpu.VMEM((8, 3 * D), f32),
                pltpu.SemaphoreType.DMA(()),
            ],
        ),
        out_shape=[
            out_of((D, 8 * D + 128), bf16),
            out_of((mbs, 8, ROWS, 3 * D), bf16),
        ],
        compiler_params=pltpu.CompilerParams(vmem_limit_bytes=VMEM_BYTES),
        cost_estimate=pl.CostEstimate(
            flops=2 * mbs * 8 * ROWS * D * 5 * D, bytes_accessed=60 << 20, transcendentals=0
        ),
        name="temporal_backward",
    )(
        slot, tokens, other, packed, probs, back_own, back_other, vec, weights,
        space_sums, mlp_sums, hidden_sums, space,
    )


def input_grad_kernel(own, *refs):
    tokens_ref, gpack_ref, vec_ref, win_ref = refs[1:5]
    out_ref, pad_s = refs[-2:]
    pad_s[...] = jnp.zeros_like(pad_s)
    for f in range(PAIR):
        pad_s[f, :PATCHES] = tokens_ref[f]
    n, r = norm_parts(pad_s[...].reshape(TILE, D).astype(f32))
    a = nt(gpack_ref[...].reshape(TILE, 3 * D), win_ref[...])
    back = norm_back(a, n, r, row_of(vec_ref, T_GAIN)).reshape(PAIR, ROWS, D)
    if own:
        back = back + refs[5][...]
        for f in range(PAIR):
            out_ref[f] = back[f, :PATCHES].astype(bf16)
    else:
        out_ref[...] = back.astype(bf16)


def input_grad(own, slot, tokens, gpack, vec, weights, extra, frames):
    mbs = gpack.shape[0]
    near = frames // PAIR
    half = 0 if own else near
    single = pl.BlockSpec((None, PAIR, ROWS, D), lambda m, i, s: (m, i, 0, 0))
    outer = pl.BlockSpec((None, None, PAIR, PATCHES, D), lambda m, i, s: (m, s[0], i, 0, 0))
    other = pl.BlockSpec((None, PAIR, PATCHES, D), lambda m, i, s: (m, i, 0, 0))

    def kernel(*refs):
        input_grad_kernel(own, *refs)

    return pl.pallas_call(
        kernel,
        grid_spec=pltpu.PrefetchScalarGridSpec(
            num_scalar_prefetch=1,
            grid=(mbs, near),
            in_specs=[
                outer if own else other,
                pl.BlockSpec((None, PAIR, ROWS, 3 * D), lambda m, i, s: (m, half + i, 0, 0)),
                fixed((16, D)),
                fixed((D, 3 * D)),
            ]
            + [single] * len(extra),
            out_specs=outer if own else single,
            scratch_shapes=[pltpu.VMEM((PAIR, ROWS, D), bf16)],
        ),
        out_shape=out_of(tokens.shape if own else (mbs, frames, ROWS, D), bf16),
        compiler_params=pltpu.CompilerParams(vmem_limit_bytes=VMEM_BYTES),
        cost_estimate=pl.CostEstimate(
            flops=2 * mbs * frames * ROWS * D * 3 * D, bytes_accessed=20 << 20, transcendentals=0
        ),
        name="input_grad",
    )(slot, tokens, gpack, vec, weights, *extra)


def last_sum_kernel(slot_ref, time_grad_ref, back_ref, patch_in_ref, patch_ref):
    del patch_in_ref
    whole = time_grad_ref[...] + back_ref[...].astype(f32)
    for f in range(PAIR):
        patch_ref[f] = whole[f, :PATCHES].astype(bf16)


def last_sum(slot, time_grad, back, patch):
    mbs, frames = time_grad.shape[:2]
    single = pl.BlockSpec((None, PAIR, ROWS, D), lambda m, i, s: (m, i, 0, 0))
    return pl.pallas_call(
        last_sum_kernel,
        grid_spec=pltpu.PrefetchScalarGridSpec(
            num_scalar_prefetch=1,
            grid=(mbs, frames // PAIR),
            in_specs=[single, single, pl.BlockSpec(memory_space=pl.ANY)],
            out_specs=pl.BlockSpec(
                (None, None, PAIR, PATCHES, D), lambda m, i, s: (m, s[1], i, 0, 0)
            ),
        ),
        out_shape=out_of(patch.shape, bf16),
        input_output_aliases={3: 0},
        name="last_sum",
    )(slot, time_grad, back, patch)


AXES = ("clip", "frame")


def swap(values):
    return lax.ppermute(values, "frame", [(0, 1), (1, 0)])


def gather(values):
    return lax.all_gather(values, AXES, axis=0, tiled=True)


def scatter_sum(values):
    return lax.psum_scatter(values, AXES, scatter_dimension=0, tiled=True)


def paired_body(
    patch_tokens, live_slots, out_grad,
    temporal_gain, temporal_shift, temporal_in, temporal_out, temporal_bias,
    spatial_gain, spatial_shift, spatial_in, spatial_out, spatial_bias,
    mlp_gain, mlp_shift, expand_weight, expand_bias, shrink_weight, shrink_bias,
):
    rows = temporal_in.shape[0]
    mine = lax.axis_index("frame")
    slot = jnp.stack([mine, 1 - mine]).astype(jnp.int32)
    sent = lax.dynamic_index_in_dim(patch_tokens, 1 - mine, 1, keepdims=False)
    other = swap(sent)

    columns = [
        v[:, None]
        for v in (
            temporal_gain, temporal_shift, temporal_bias, spatial_gain, spatial_shift,
            spatial_bias, mlp_gain, mlp_shift, shrink_bias,
        )
    ] + [expand_bias.reshape(rows, CHUNKS)]
    columns = jnp.concatenate(columns, axis=1)
    columns = jnp.pad(columns, ((0, 0), (0, 128 - columns.shape[1])))
    first = gather(jnp.concatenate([temporal_in, columns], axis=1))
    second = gather(jnp.concatenate([spatial_in, temporal_out, spatial_out], axis=1))
    turned = expand_weight.reshape(rows, D, CHUNKS).transpose(0, 2, 1).reshape(rows, CHUNKS * D)
    third = gather(
        jnp.concatenate([turned, shrink_weight.reshape(rows, CHUNKS * D)], axis=1)
    )
    vec = first[:, 3 * D :].T[:16].astype(f32)
    hidden = vec[HIDDEN : HIDDEN + CHUNKS].reshape(1, CHUNKS * D)

    mbs, frames = patch_tokens.shape[0], patch_tokens.shape[2]
    packed_t, probs_t, mixed_own, mixed_other = temporal_forward(
        slot, patch_tokens, other, vec, first
    )
    mixed_here = swap(mixed_other)
    saved = spatial_forward(0, slot, patch_tokens, mixed_own, vec, second, ())
    saved = spatial_forward(1, slot, patch_tokens, mixed_here, vec, second, saved)
    time, packed_s, probs_s, mixed_s, space = saved

    live = (slot[:, None] < live_slots[:, 0][None, :]).astype(jnp.int32)
    live = jnp.repeat(live.reshape(-1), frames // PAIR)
    block_out, space_grad, g_mlp, sums_m, sums_h = mlp(
        slot, live, space, out_grad, vec, hidden, third
    )
    g_mlp = scatter_sum(g_mlp)

    kept = (space_grad, packed_s, probs_s, mixed_s, time)
    g_far, sums_s, time_grad_far, back_far = spatial_backward(
        1, *kept, mixed_here, vec, second, ()
    )
    back_other = swap(back_far)
    g_space, sums_s, time_grad_own, back_own = spatial_backward(
        0, *kept, mixed_own, vec, second, (g_far, sums_s)
    )
    g_rest, gpack = temporal_backward(
        slot, patch_tokens, other, packed_t, probs_t, back_own, back_other, vec, first,
        sums_s, sums_m, sums_h, g_space,
    )
    g_rest, g_mlp = lax.optimization_barrier((g_rest, g_mlp))
    g_rest = scatter_sum(g_rest)
    send = input_grad(False, slot, other, gpack, vec, first, (), frames)
    patch_grad = input_grad(
        True, slot, patch_tokens, gpack, vec, first, (time_grad_own,), frames
    )
    patch_grad = last_sum(slot, time_grad_far, swap(send), patch_grad)

    g_rest, g_mlp = g_rest.astype(f32), g_mlp.astype(f32)
    tail, g_space = g_rest[:, 3 * D : 3 * D + 128], g_rest[:, 3 * D + 128 :]

    def vector(at):
        return tail[:, at]

    wide = CHUNKS * D
    g_expand = g_mlp[:, :wide].reshape(rows, CHUNKS, D).transpose(0, 2, 1).reshape(rows, wide)
    return (
        block_out,
        patch_grad,
        vector(T_GAIN),
        vector(T_SHIFT),
        g_rest[:, : 3 * D],
        g_space[:, 4 * D :],
        vector(T_BIAS),
        vector(S_GAIN),
        vector(S_SHIFT),
        g_space[:, : 3 * D],
        g_space[:, 3 * D : 4 * D],
        vector(S_BIAS),
        vector(M_GAIN),
        vector(M_SHIFT),
        g_expand,
        tail[:, HIDDEN : HIDDEN + CHUNKS].reshape(rows * CHUNKS),
        g_mlp[:, wide:].reshape(rows * CHUNKS, D),
        vector(M_BIAS),
    )


def body(*args):
    tokens, temporal_in, expand_weight = args[0], args[5], args[15]
    paired = (
        lax.axis_size("frame") == 2
        and tokens.shape[1:] == (2, 4, PATCHES, D)
        and temporal_in.shape[1] == 3 * D
        and expand_weight.shape[1] == CHUNKS * CHUNK
    )
    return paired_body(*args) if paired else generic_body(*args)


def solution(mesh):
    placed = (
        P(None, "clip", "frame", None, None),
        P(None, "clip"),
        P(None, "clip", "frame", None, None),
        P(("clip", "frame")),
        P(("clip", "frame")),
        P(("clip", "frame"), None),
        P(("clip", "frame"), None),
        P(("clip", "frame")),
        P(("clip", "frame")),
        P(("clip", "frame")),
        P(("clip", "frame"), None),
        P(("clip", "frame"), None),
        P(("clip", "frame")),
        P(("clip", "frame")),
        P(("clip", "frame")),
        P(("clip", "frame"), None),
        P(("clip", "frame")),
        P(("clip", "frame"), None),
        P(("clip", "frame")),
    )
    return jax.shard_map(
        body,
        mesh=mesh,
        in_specs=placed,
        out_specs=(
            P(None, "clip", "frame", None, None),
            P(None, "clip", "frame", None, None),
            P(("clip", "frame")),
            P(("clip", "frame")),
            P(("clip", "frame"), None),
            P(("clip", "frame"), None),
            P(("clip", "frame")),
            P(("clip", "frame")),
            P(("clip", "frame")),
            P(("clip", "frame"), None),
            P(("clip", "frame"), None),
            P(("clip", "frame")),
            P(("clip", "frame")),
            P(("clip", "frame")),
            P(("clip", "frame"), None),
            P(("clip", "frame")),
            P(("clip", "frame"), None),
            P(("clip", "frame")),
        ),
        check_vma=False,
    )
```
